32 devices in a mesh: row: 4 (over z), col: 8 (over y, x, core).
Axes of the slice: x: 2, y: 2, z: 4, core: 2. Of those that a mesh axis runs over, the one named last changes fastest.
Arguments:
- right_side: float32 [2, 16, 512, 512], P(None, None, 'row', 'col'), may hold values from -12 to 12
- symbol: float32 [1024, 1024, 256], P('col', 'row'), may hold values from -0.25 to 4.75, as said below
Outputs:
- solution_field: float32 [2, 16, 512, 512], P(None, None, 'row', 'col')
- residual: float32 [2, 16, 512, 512], P(None, None, 'row', 'col')
The draws below stay inside these ranges and needn't reach their ends.
Inputs may be any that keep to these rules, and one draw needn't show every extreme that they name: For each frequency pair (u, v) the 16 x 16 matrix with entries symbol[u, v, s * 16 + t] is symmetric and positive definite.
All inputs are finite; a program needn't handle non-finite values.
Results may differ from the reference program's by a relative error of at most 0.0003.
Values sent between devices are 32-bit elements; how exact they have to be, the bound alone decides.
A program may use at most 576 MiB of HBM per device.

```python
import math
import jax
import jax.numpy as jnp

BR = 512
BC = 512
SEG = 16
NRHS = 2
ITERS = 1
PR = 1024
PC = 1024


def draw_right_side(key, part):
    rows = jnp.arange(BR, dtype=jnp.float32)[:, None] / max(BR - 1, 1)
    cols = jnp.arange(BC, dtype=jnp.float32)[None, :] / max(BC - 1, 1)
    scale = 1.0 + rows + cols
    shape = (NRHS, SEG, BR, BC)
    base = jnp.clip(jax.random.normal(key, shape, jnp.float32), -4.0, 4.0)
    return base * scale


def draw_symbol(key, part):
    first, second, third = jax.random.split(key, 3)
    shape = (PR, PC, SEG, SEG)
    raw = jax.random.uniform(first, shape, jnp.float32, -1.0, 1.0)
    paired = 0.5 * (raw + jnp.transpose(raw, (0, 1, 3, 2)))
    unit = jnp.eye(SEG, dtype=jnp.float32)[None, None, :, :]
    lifted = jax.random.uniform(second, (PR, PC, SEG, 1), jnp.float32, 1.0, 4.0)
    block = paired * (1.0 - unit) + unit * (SEG - 1.0 + lifted)
    level = jnp.exp(jax.random.uniform(third, (PR, PC), jnp.float32, math.log(0.5), math.log(4.0)))
    return (block * level[:, :, None, None] / SEG).reshape(PR, PC, SEG * SEG)


def setup_inputs(seed: int = 0) -> dict:
    keys = jax.random.split(jax.random.key(seed), 3)
    right_side = draw_right_side(jax.random.fold_in(keys[2], 71), 0)
    symbol = draw_symbol(jax.random.fold_in(keys[2], 71), 0)
    return {"right_side": right_side, "symbol": symbol}


def operate(vector_in, symbol):
    padded = jnp.pad(vector_in, ((0, 0), (0, PR - BR), (0, PC - BC)))
    spectrum = jnp.fft.fft2(padded)
    real_part = jnp.real(spectrum)
    imag_part = jnp.imag(spectrum)
    blocks = symbol.reshape(PR, PC, SEG, SEG)
    mixed_real = jnp.stack([jnp.sum(jnp.transpose(blocks[:, :, index, :], (2, 0, 1)) * real_part, axis=0) for index in range(SEG)])
    mixed_imag = jnp.stack([jnp.sum(jnp.transpose(blocks[:, :, index, :], (2, 0, 1)) * imag_part, axis=0) for index in range(SEG)])
    restored = jnp.fft.ifft2(mixed_real + 1j * mixed_imag)
    return jnp.real(restored)[:, :BR, :BC]


def reference(right_side, symbol):
    solutions = []
    residuals = []
    for index in range(NRHS):
        solution = jnp.zeros_like(right_side[index])
        residual = right_side[index]
        direction = right_side[index]
        norm_now = jnp.sum(residual * residual)
        for iteration in range(ITERS):
            applied = operate(direction, symbol)
            step_size = norm_now / jnp.sum(direction * applied)
            solution = solution + step_size * direction
            residual = residual - step_size * applied
            fresh = jnp.sum(residual * residual)
            direction = residual + (fresh / norm_now) * direction
            norm_now = fresh
        solutions.append(solution)
        residuals.append(residual)
    return jnp.stack(solutions), jnp.stack(residuals)
```

```python
import math

import jax
import jax.numpy as jnp
from jax import lax
from jax.experimental import pallas as pl
from jax.experimental.pallas import tpu as pltpu
from jax.sharding import PartitionSpec as P

PRECISION = lax.Precision.HIGH
ROW_STEP = 8


def tables(phase, length):
    angle = (phase % length).astype(jnp.float32) * (2.0 * math.pi / length)
    return lax.optimization_barrier((jnp.cos(angle), jnp.sin(angle)))


def steps(count, stride=1):
    return jnp.arange(count, dtype=jnp.int32) * stride


def row_transform(freq_rows, rows_all, freq_block):
    fine = math.gcd(32, freq_block)
    place = jnp.tile(steps(rows_all), 2)
    part_in = jnp.repeat(steps(2), rows_all)
    coarse_cos, coarse_sin = tables(steps(freq_rows // fine, fine)[:, None] * place[None, :], freq_rows)
    quarter = (steps(2)[:, None] - part_in[None, :]) * (freq_rows // 4) + freq_rows
    fine_cos, fine_sin = tables(
        steps(fine)[None, :, None] * place[None, None, :] + quarter[:, None, :], freq_rows
    )
    shape = (freq_rows // freq_block, 1, freq_block // fine, 1, 2 * rows_all)
    coarse_cos, coarse_sin = coarse_cos.reshape(shape), coarse_sin.reshape(shape)
    fine_cos, fine_sin = fine_cos[None, :, None], fine_sin[None, :, None]
    return (coarse_cos * fine_cos - coarse_sin * fine_sin).reshape(2 * freq_rows, 2 * rows_all)


def col_transform(freq_cols, cols_all, freq_block, first):
    fine = math.gcd(16, cols_all)
    freq = first + steps(freq_block)
    coarse_cos, coarse_sin = tables(steps(cols_all // fine, fine)[:, None] * freq[None, :], freq_cols)
    quarter = steps(2, freq_cols // 4)[:, None, None]
    fine_cos, fine_sin = tables(steps(fine)[None, :, None] * freq[None, None, :] + quarter, freq_cols)
    coarse_cos, coarse_sin = coarse_cos[None, :, None], coarse_sin[None, :, None]
    fine_cos, fine_sin = fine_cos[:, None], fine_sin[:, None]
    return (coarse_cos * fine_cos - coarse_sin * fine_sin).reshape(2, cols_all, freq_block)


def mix(symbol, spectra, rhs_count, seg_count):
    freq_rows, freq_cols, pair_count = symbol.shape
    devices, parts, _, width = spectra[0].shape
    count = len(spectra)
    share = width // freq_cols
    step = math.gcd(ROW_STEP, freq_rows)

    def place(field):
        owner, at = divmod(field, share * count)
        group, at = divmod(at, share)
        return group, owner, slice(at * freq_cols, (at + 1) * freq_cols)

    def body(symbol_ref, *refs):
        in_refs, out_refs, turned = refs[:count], refs[count : 2 * count], refs[2 * count]

        def one(u, carry):
            turned[...] = symbol_ref[u].T
            sums = {}
            for t in range(seg_count):
                column = turned[t * seg_count : (t + 1) * seg_count, :]
                for part in range(parts):
                    for k in range(rhs_count):
                        group, owner, lanes = place(k * seg_count + t)
                        term = column * in_refs[group][owner, part, pl.ds(u, 1), lanes]
                        sums[part, k] = sums[part, k] + term if t else term
            for part in range(parts):
                for k in range(rhs_count):
                    for s in range(seg_count):
                        group, owner, lanes = place(k * seg_count + s)
                        out_refs[group][owner, part, pl.ds(u, 1), lanes] = sums[part, k][s : s + 1, :]
            return carry

        lax.fori_loop(0, step, one, 0)

    block = pl.BlockSpec((devices, parts, step, width), lambda i: (0, 0, i, 0))
    return pl.pallas_call(
        body,
        grid=(freq_rows // step,),
        in_specs=[pl.BlockSpec((step, freq_cols, pair_count), lambda i: (i, 0, 0))] + [block] * count,
        out_specs=[block] * count,
        out_shape=[jax.ShapeDtypeStruct(spectra[0].shape, jnp.float32)] * count,
        scratch_shapes=[pltpu.VMEM((pair_count, freq_cols), jnp.float32)],
        name="mix",
    )(symbol, *spectra)


def local(right_side, symbol):
    row_count = lax.axis_size("row")
    col_count = lax.axis_size("col")
    rhs_count, seg_count, row_block, col_block = right_side.shape
    freq_block, freq_width = symbol.shape[:2]
    rows_all = row_block * row_count
    cols_all = col_block * col_count
    freq_rows = freq_block * col_count
    freq_cols = freq_width * row_count
    fields = rhs_count * seg_count
    held = fields // col_count
    to_rows = row_transform(freq_rows, rows_all, freq_block)
    to_cols = col_transform(freq_cols, cols_all, freq_width, lax.axis_index("row") * freq_width)
    count = math.gcd(2, held)
    share = held // count
    norm_factor = 1.0 / (freq_rows * freq_cols)
    flat = right_side.reshape(fields, row_block, col_block)
    whole_cols = lax.all_to_all(flat, "col", split_axis=0, concat_axis=2, tiled=True)
    spectra = []
    for group in range(count):
        own = whole_cols[group * share : (group + 1) * share]
        whole = lax.all_gather(own, "row", axis=1, tiled=True)
        half = jnp.einsum("prc,zcv->zrpv", whole, to_cols, precision=PRECISION)
        half = half.reshape(2 * rows_all, share * freq_width)
        spectrum = jnp.dot(to_rows, half, precision=PRECISION)
        spectrum = spectrum.reshape(col_count, 2, freq_block, share * freq_width)
        spectra.append(lax.all_to_all(spectrum, "col", split_axis=0, concat_axis=0, tiled=True))
    mixtures = mix(symbol, spectra, rhs_count, seg_count)
    sums = []
    for spectrum, mixed in zip(spectra, mixtures):
        for at in range(share):
            lanes = slice(at * freq_width, (at + 1) * freq_width)
            sums.append(jnp.sum(spectrum[..., lanes] * mixed[..., lanes], axis=(1, 2, 3)))
    curve = jnp.stack(sums, axis=1).reshape(rhs_count, seg_count).sum(axis=1) * norm_factor
    norm_now = jnp.sum(right_side * right_side, axis=(1, 2, 3))
    norm_now, curve = lax.psum((norm_now, curve), ("row", "col"))
    images = []
    for mixed in mixtures:
        mixed = lax.all_to_all(mixed, "col", split_axis=0, concat_axis=0, tiled=True)
        mixed, norm_now, curve = lax.optimization_barrier((mixed, norm_now, curve))
        mixed = mixed.reshape(2 * freq_rows, share * freq_width)
        back = lax.dot_general(to_rows, mixed, (((0,), (0,)), ((), ())), precision=PRECISION)
        back = back.reshape(2, rows_all, share, freq_width)
        image = jnp.einsum("zrpv,zcv->prc", back, to_cols, precision=PRECISION)
        images.append(lax.psum_scatter(image, "row", scatter_dimension=1, tiled=True))
    image = jnp.concatenate(images, axis=0)
    applied = lax.all_to_all(image, "col", split_axis=2, concat_axis=0, tiled=True)
    applied = applied.reshape(right_side.shape) * norm_factor
    step_size = (norm_now / curve)[:, None, None, None]
    return (step_size * right_side, right_side - step_size * applied)


MESH = pl.DeviceIdType.MESH
VMEM_LIMIT = 60 * 1024 * 1024


def split(value):
    high = value.astype(jnp.bfloat16)
    return high, (value - high.astype(jnp.float32)).astype(jnp.bfloat16)


def product(left, right):
    def one(a, b):
        return jnp.dot(a, b, preferred_element_type=jnp.float32)

    return one(left[0], right[0]) + (one(left[1], right[0]) + one(left[0], right[1]))


class Place:
    def __init__(self, ring, pair):
        self.ring, self.pair = ring, pair
        self.at, self.me = lax.axis_index("row"), lax.axis_index("col")
        self.core, self.x, self.y = self.me % 2, (self.me // 2) % 2, self.me // 4

    def beside(self, flip_core, flip_x, flip_y):
        core = self.core + flip_core * (1 - 2 * self.core)
        x = self.x + flip_x * (1 - 2 * self.x)
        y = self.y + flip_y * (1 - 2 * self.y)
        return core, x, y, y * 4 + x * 2 + core

    def partner(self, kind, turn):
        return self.beside(turn % 2, (turn // 2) * (1 - kind), (turn // 2) * kind)

    def layer(self, kind, core, x, y):
        return ((kind * 2 + x * (1 - kind) + y * kind) * 2 + core) * self.pair

    def ahead(self, way):
        return (self.at + 1 + (self.ring - 2) * way) % self.ring

    def peers(self):
        return [self.beside(bit % 2, (bit // 2) % 2, bit // 4) for bit in range(1, 8)]

    def greet(self):
        barrier = pltpu.get_barrier_semaphore()
        others = [(self.at, peer[3]) for peer in self.peers()]
        others += [(self.ahead(way), self.me) for way in range(2)]
        for other in others:
            pl.semaphore_signal(barrier, inc=1, device_id=other, device_id_type=MESH)
        pl.semaphore_wait(barrier, len(others))


def rows_of(at, size):
    return pl.ds(pl.multiple_of(at * size, size), size)


def arrived(ref, sem):
    pltpu.make_async_copy(ref, ref, sem).wait()


def send(src, dst, send_sem, recv_sem, row, col):
    return pltpu.make_async_remote_copy(
        src_ref=src, dst_ref=dst, send_sem=send_sem, recv_sem=recv_sem,
        device_id=(row, col), device_id_type=MESH,
    )


def forward_call(packed, fine, coarse, to_cols, ring, freq_block, freq_width):
    rhs_count, seg_count, col_block, row_block = packed.shape
    pair = seg_count // 8
    fields = rhs_count * 2 * pair
    rows_all, cols_all = row_block * ring, col_block * 8

    def body(packed, fine, coarse, to_cols, spec, stage, pix, high, low, half_high, half_low, out,
             in_send, in_recv, near_send, near_recv, far_send, far_recv, out_send, out_recv):
        here = Place(ring, pair)
        here.greet()
        own = rows_of(here.at, row_block)
        entry = []
        for k in range(rhs_count):
            for kind in range(2):
                slot = k * 2 + kind
                dst = stage.at[pl.ds(slot * pair, pair), rows_of(here.me, col_block)]
                for n, (core, x, y, peer) in enumerate(here.peers()):
                    src = packed.at[k, pl.ds(here.layer(kind, core, x, y), pair)]
                    copy = send(src, dst, in_send.at[slot, n], in_recv.at[slot], here.at, peer)
                    copy.start()
                    entry.append(copy)
                mine = packed.at[k, pl.ds(here.layer(kind, here.core, here.x, here.y), pair)]
                pltpu.make_async_copy(mine, dst, in_recv.at[slot]).start()

        def build(i, carry):
            cos_c, sin_c = coarse[0, pl.ds(i, 1), :], coarse[1, pl.ds(i, 1), :]
            cos_f, sin_f = fine[0], fine[1]
            cos = split(cos_c * cos_f - sin_c * sin_f)
            sin = split(sin_c * cos_f + cos_c * sin_f)
            for part, table in ((0, high), (1, low)):
                table[i, :freq_block, :rows_all] = cos[part]
                table[i, :freq_block, rows_all:] = sin[part]
                table[i, freq_block:, :rows_all] = -sin[part]
                table[i, freq_block:, rows_all:] = cos[part]
            return carry

        lax.fori_loop(0, 8, build, 0)

        def near(f, way):
            return send(pix.at[f, own], pix.at[f, own], near_send.at[way, f], near_recv.at[way, f],
                        here.ahead(way), here.me)

        def far(f):
            way = f % 2
            block = pix.at[f, rows_of(here.ahead(1 - way), row_block)]
            return send(block, block, far_send.at[f], far_recv.at[f], here.ahead(way), here.me)

        def enter(f):
            @pl.when(f % pair == 0)
            def _():
                arrived(stage.at[pl.ds(f, pair)], in_recv.at[f // pair])

            pix[f, own] = stage[f].T
            near(f, 0).start()
            near(f, 1).start()

        def relay(f):
            way = f % 2
            arrived(pix.at[f, rows_of(here.ahead(1 - way), row_block)], near_recv.at[way, f])
            far(f).start()

        def leave(f, turn):
            k, kind, j, slot = f // (2 * pair), (f // pair) % 2, f % pair, f % 2
            peer = here.partner(kind, turn)[3]
            dst = spec.at[k, here.layer(kind, here.core, here.x, here.y) + j]
            src = out.at[slot, turn]
            if turn == 0:
                return pltpu.make_async_copy(src, dst, out_send.at[f, 0])
            return send(src, dst, out_send.at[f, turn], out_recv.at[f, turn], here.at, peer)

        def sent(f):
            leave(f, 0).wait()
            for turn in range(1, 4):
                leave(f, turn).wait_send()

        def compute(f):
            way = f % 2
            arrived(pix.at[f, rows_of(here.ahead(way), row_block)], near_recv.at[1 - way, f])
            arrived(pix.at[f, rows_of((here.at + 2) % ring, row_block)], far_recv.at[f])
            half = product(split(pix[f]), (to_cols[0], to_cols[1]))
            for part in range(2):
                at = slice(part * rows_all, (part + 1) * rows_all)
                half_high[at, :], half_low[at, :] = split(half[:, part * freq_width : (part + 1) * freq_width])

            @pl.when(f >= 2)
            def _():
                sent(f - 2)

            kind, slot = (f // pair) % 2, f % 2
            right = (half_high[...], half_low[...])
            for turn in (1, 2, 3, 0):
                table = kind * 4 + turn
                value = product((high[table], low[table]), right)
                out[slot, turn] = value.reshape(2, freq_block, freq_width)
                leave(f, turn).start()

        enter(0)
        enter(1)
        relay(0)

        def step(f, carry):
            @pl.when(f + 2 < fields)
            def _():
                enter(f + 2)

            @pl.when(f + 1 < fields)
            def _():
                relay(f + 1)

            compute(f)
            return carry

        lax.fori_loop(0, fields, step, 0)
        sent(fields - 2)
        sent(fields - 1)
        for copy in entry:
            copy.wait_send()

        def finish(f, carry):
            near(f, 0).wait_send()
            near(f, 1).wait_send()
            far(f).wait_send()
            for turn in range(1, 4):
                leave(f, turn).wait_recv()
            return carry

        lax.fori_loop(0, fields, finish, 0)

    dma = pltpu.SemaphoreType.DMA
    vmem = pl.BlockSpec(memory_space=pltpu.VMEM)
    hbm = pl.BlockSpec(memory_space=pl.ANY)
    return pl.pallas_call(
        body,
        in_specs=[hbm, vmem, vmem, vmem],
        out_specs=hbm,
        out_shape=jax.ShapeDtypeStruct((rhs_count, seg_count, 2, freq_block, freq_width), jnp.float32),
        scratch_shapes=[
            pltpu.VMEM((fields, cols_all, row_block), jnp.float32),
            pltpu.VMEM((fields, rows_all, cols_all), jnp.float32),
            pltpu.VMEM((8, 2 * freq_block, 2 * rows_all), jnp.bfloat16),
            pltpu.VMEM((8, 2 * freq_block, 2 * rows_all), jnp.bfloat16),
            pltpu.VMEM((2 * rows_all, freq_width), jnp.bfloat16),
            pltpu.VMEM((2 * rows_all, freq_width), jnp.bfloat16),
            pltpu.VMEM((2, 4, 2, freq_block, freq_width), jnp.float32),
            dma((rhs_count * 2, 7)), dma((rhs_count * 2,)),
            dma((2, fields)), dma((2, fields)), dma((fields,)), dma((fields,)),
            dma((fields, 4)), dma((fields, 4)),
        ],
        compiler_params=pltpu.CompilerParams(
            collective_id=0, has_side_effects=True, vmem_limit_bytes=VMEM_LIMIT
        ),
        name="forward",
    )(packed, fine, coarse, to_cols)


def backward_call(mixed, fine, coarse, from_cols, ring, row_block, col_block):
    rhs_count, seg_count, _, freq_block, freq_width = mixed.shape
    pair = seg_count // 8
    fields = rhs_count * 2 * pair
    rows_all, cols_all = row_block * ring, col_block * 8

    def body(mixed, fine, coarse, from_cols, image, got, part_sum, high, low, half_high, half_low,
             chain_in, chain_out, side_in, turned,
             in_send, in_recv, chain_send, chain_recv, pass_send, pass_recv, side_send, side_recv,
             out_send, out_recv):
        here = Place(ring, pair)
        here.greet()

        def enter(f, turn):
            k, kind, j = f // (2 * pair), (f // pair) % 2, f % pair
            core, x, y, peer = here.partner(kind, turn)
            src, dst = mixed.at[k, here.layer(kind, core, x, y) + j], got.at[f, turn]
            if turn == 0:
                return pltpu.make_async_copy(src, dst, in_recv.at[f, 0])
            return send(src, dst, in_send.at[f, turn], in_recv.at[f, turn], here.at, peer)

        def begin(f, carry):
            for turn in (1, 2, 3, 0):
                enter(f, turn).start()
            return carry

        lax.fori_loop(0, fields, begin, 0)

        def build(i, carry):
            kind, turn = i // 4, i % 4
            cos_f, sin_f = fine[0], fine[1]
            cos_c, sin_c = coarse[0, i], coarse[1, i]
            cos = split(cos_c * cos_f - sin_c * sin_f)
            sin = split(sin_c * cos_f + cos_c * sin_f)
            for part, table in ((0, high), (1, low)):
                for block in range(2):
                    first = pl.multiple_of((turn * 2 + block) * freq_block, freq_block)
                    lanes = pl.ds(first, freq_block)
                    table[kind, :rows_all, lanes] = -sin[part] if block else cos[part]
                    table[kind, rows_all:, lanes] = cos[part] if block else sin[part]
            return carry

        lax.fori_loop(0, 8, build, 0)

        def block_of(f, at):
            return part_sum.at[f, rows_of(at, row_block)]

        def chain(f):
            way = f % 2
            return send(block_of(f, (here.at + 2) % ring), chain_in.at[f],
                        chain_send.at[f], chain_recv.at[f], here.ahead(way), here.me)

        def side(f):
            back = here.ahead(1 - f % 2)
            return send(block_of(f, back), side_in.at[f], side_send.at[f], side_recv.at[f], back, here.me)

        def onward(f):
            front = here.ahead(f % 2)
            return send(block_of(f, front), chain_out.at[f], pass_send.at[f], pass_recv.at[f], front, here.me)

        def compute(f):
            for turn in range(4):
                arrived(got.at[f, turn], in_recv.at[f, turn])
            kind = (f // pair) % 2
            spectrum = split(got[f].reshape(8 * freq_block, freq_width))
            half = product((high[kind], low[kind]), spectrum)
            for part in range(2):
                at = slice(part * freq_width, (part + 1) * freq_width)
                half_high[:, at], half_low[:, at] = split(half[part * rows_all : (part + 1) * rows_all])
            part_sum[f] = product((half_high[...], half_low[...]), (from_cols[0], from_cols[1]))
            chain(f).start()
            side(f).start()

        def relay(f):
            front = rows_of(here.ahead(f % 2), row_block)
            arrived(chain_in.at[f], chain_recv.at[f])
            part_sum[f, front] = part_sum[f, front] + chain_in[f]
            onward(f).start()

        def leave(f, n, peer):
            k, kind, j = f // (2 * pair), (f // pair) % 2, f % pair
            half = here.y * (1 - kind) + here.x * kind
            dst = image.at[k, here.layer(kind, here.core, here.x, here.y) + j, half]
            src = turned.at[f, rows_of(peer, col_block)]
            if n == 0:
                return pltpu.make_async_copy(src, dst, out_send.at[f, 0])
            return send(src, dst, out_send.at[f, n], out_recv.at[f, n], here.at, peer)

        others = [here.me] + [peer[3] for peer in here.peers()]

        def final(f):
            arrived(chain_out.at[f], pass_recv.at[f])
            arrived(side_in.at[f], side_recv.at[f])
            own = rows_of(here.at, row_block)
            turned[f] = (part_sum[f, own] + (chain_out[f] + side_in[f])).T
            for n, peer in enumerate(others):
                leave(f, n, peer).start()

        def step(f, carry):
            @pl.when(f < fields)
            def _():
                compute(f)

            @pl.when((f >= 1) & (f < fields + 1))
            def _():
                relay(f - 1)

            @pl.when(f >= 2)
            def _():
                final(f - 2)

            return carry

        lax.fori_loop(0, fields + 2, step, 0)

        def finish(f, carry):
            for turn in range(1, 4):
                enter(f, turn).wait_send()
            chain(f).wait_send()
            side(f).wait_send()
            onward(f).wait_send()
            leave(f, 0, here.me).wait()
            for n, peer in enumerate(others):
                if n:
                    leave(f, n, peer).wait()
            return carry

        lax.fori_loop(0, fields, finish, 0)

    dma = pltpu.SemaphoreType.DMA
    vmem = pl.BlockSpec(memory_space=pltpu.VMEM)
    hbm = pl.BlockSpec(memory_space=pl.ANY)
    block = (fields, row_block, cols_all)
    return pl.pallas_call(
        body,
        in_specs=[hbm, vmem, vmem, vmem],
        out_specs=hbm,
        out_shape=jax.ShapeDtypeStruct((rhs_count, seg_count, 2, col_block, row_block), jnp.float32),
        scratch_shapes=[
            pltpu.VMEM((fields, 4, 2, freq_block, freq_width), jnp.float32),
            pltpu.VMEM((fields, rows_all, cols_all), jnp.float32),
            pltpu.VMEM((2, 2 * rows_all, 8 * freq_block), jnp.bfloat16),
            pltpu.VMEM((2, 2 * rows_all, 8 * freq_block), jnp.bfloat16),
            pltpu.VMEM((rows_all, 2 * freq_width), jnp.bfloat16),
            pltpu.VMEM((rows_all, 2 * freq_width), jnp.bfloat16),
            pltpu.VMEM(block, jnp.float32), pltpu.VMEM(block, jnp.float32), pltpu.VMEM(block, jnp.float32),
            pltpu.VMEM((fields, cols_all, row_block), jnp.float32),
            dma((fields, 4)), dma((fields, 4)),
            dma((fields,)), dma((fields,)), dma((fields,)), dma((fields,)), dma((fields,)), dma((fields,)),
            dma((fields, 8)), dma((fields, 8)),
        ],
        compiler_params=pltpu.CompilerParams(
            collective_id=1, has_side_effects=True, vmem_limit_bytes=VMEM_LIMIT
        ),
        name="backward",
    )(mixed, fine, coarse, from_cols)


def mix_all(symbol, spectra):
    freq_rows, freq_cols, pair_count = symbol.shape
    rhs_count, seg_count, parts = spectra.shape[:3]
    step = math.gcd(ROW_STEP, freq_rows)

    def body(symbol_ref, in_ref, out_ref, curve_ref, turned):
        def one(u, carry):
            turned[...] = symbol_ref[u].T
            sums = {}
            for t in range(seg_count):
                column = turned[t * seg_count : (t + 1) * seg_count, :]
                for part in range(parts):
                    for k in range(rhs_count):
                        term = column * in_ref[k, t, part, pl.ds(u, 1), :]
                        sums[part, k] = sums[part, k] + term if t else term
            for part in range(parts):
                for k in range(rhs_count):
                    for s in range(seg_count):
                        out_ref[k, s, part, pl.ds(u, 1), :] = sums[part, k][s : s + 1, :]
            return carry

        lax.fori_loop(0, step, one, 0)

        @pl.when(pl.program_id(0) == 0)
        def _():
            curve_ref[...] = jnp.zeros_like(curve_ref)

        for k in range(rhs_count):
            total = curve_ref[k]
            for t in range(seg_count):
                for part in range(parts):
                    total = total + in_ref[k, t, part] * out_ref[k, t, part]
            curve_ref[k] = total

    block = pl.BlockSpec((rhs_count, seg_count, parts, step, freq_cols), lambda i: (0, 0, 0, i, 0))
    return pl.pallas_call(
        body,
        grid=(freq_rows // step,),
        in_specs=[pl.BlockSpec((step, freq_cols, pair_count), lambda i: (i, 0, 0)), block],
        out_specs=[block, pl.BlockSpec((rhs_count, step, freq_cols), lambda i: (0, 0, 0))],
        out_shape=[
            jax.ShapeDtypeStruct(spectra.shape, jnp.float32),
            jax.ShapeDtypeStruct((rhs_count, step, freq_cols), jnp.float32),
        ],
        scratch_shapes=[pltpu.VMEM((pair_count, freq_cols), jnp.float32)],
        name="mix",
    )(symbol, spectra)


def halves(table):
    high = lax.reduce_precision(table, 8, 7)
    return jnp.stack([high, table - high]).astype(jnp.bfloat16)


def routed(right_side, symbol):
    ring = lax.axis_size("row")
    rhs_count, seg_count, row_block, col_block = right_side.shape
    freq_block, freq_width = symbol.shape[:2]
    rows_all, cols_all = row_block * ring, col_block * 8
    freq_rows, freq_cols = freq_block * 8, freq_width * ring
    norm_factor = 1.0 / (freq_rows * freq_cols)
    here = Place(ring, seg_count // 8)
    owners = jnp.stack([here.partner(kind, turn)[3] for kind in range(2) for turn in range(4)])
    fine = jnp.stack(tables(steps(freq_block)[:, None] * steps(rows_all)[None, :], freq_rows))
    coarse = jnp.stack(tables(owners[:, None] * steps(rows_all, freq_block)[None, :], freq_rows))
    to_cols = col_transform(freq_cols, cols_all, freq_width, lax.axis_index("row") * freq_width)
    packed = right_side.transpose(0, 1, 3, 2)
    spectra = forward_call(
        packed, fine, coarse, halves(to_cols.transpose(1, 0, 2).reshape(cols_all, 2 * freq_width)),
        ring, freq_block, freq_width,
    )
    mixed, curve = mix_all(symbol, spectra)
    curve = jnp.sum(curve, axis=(1, 2)) * norm_factor
    norm_now = jnp.sum(right_side * right_side, axis=(1, 2, 3))
    norm_now, curve = lax.psum((norm_now, curve), ("row", "col"))
    image = backward_call(
        mixed, fine.transpose(0, 2, 1), coarse[..., None],
        halves(to_cols.transpose(0, 2, 1).reshape(2 * freq_width, cols_all)), ring, row_block, col_block,
    )
    applied = (image[:, :, 0] + image[:, :, 1]).transpose(0, 1, 3, 2) * norm_factor
    step_size = (norm_now / curve)[:, None, None, None]
    return (step_size * right_side, right_side - step_size * applied)


def fits(mesh, right_side, symbol):
    ring, wide = mesh.shape["row"], mesh.shape["col"]
    _, seg_count, rows, cols = right_side.shape
    freq_rows, freq_cols = symbol.shape[:2]
    aligned = all(n % 128 == 0 for n in (rows // ring, freq_rows // wide, freq_cols // ring))
    return ring == 4 and wide == 8 and seg_count % 16 == 0 and cols // wide % 8 == 0 and aligned


def solution(mesh):
    placed = P(None, None, "row", "col")

    def whole(right_side, symbol):
        return jax.shard_map(
            routed if fits(mesh, right_side, symbol) else local,
            mesh=mesh,
            in_specs=(placed, P("col", "row", None)),
            out_specs=(placed, placed),
            check_vma=False,
        )(right_side, symbol)

    return whole
```

```python
import math

import jax
import jax.numpy as jnp
from jax import lax
from jax.experimental import pallas as pl
from jax.experimental.pallas import tpu as pltpu
from jax.sharding import PartitionSpec as P

PRECISION = lax.Precision.HIGH
ROW_STEP = 8


def tables(phase, length):
    angle = (phase % length).astype(jnp.float32) * (2.0 * math.pi / length)
    return lax.optimization_barrier((jnp.cos(angle), jnp.sin(angle)))


def steps(count, stride=1):
    return jnp.arange(count, dtype=jnp.int32) * stride


def row_transform(freq_rows, rows_all, freq_block):
    fine = math.gcd(32, freq_block)
    place = jnp.tile(steps(rows_all), 2)
    part_in = jnp.repeat(steps(2), rows_all)
    coarse_cos, coarse_sin = tables(steps(freq_rows // fine, fine)[:, None] * place[None, :], freq_rows)
    quarter = (steps(2)[:, None] - part_in[None, :]) * (freq_rows // 4) + freq_rows
    fine_cos, fine_sin = tables(
        steps(fine)[None, :, None] * place[None, None, :] + quarter[:, None, :], freq_rows
    )
    shape = (freq_rows // freq_block, 1, freq_block // fine, 1, 2 * rows_all)
    coarse_cos, coarse_sin = coarse_cos.reshape(shape), coarse_sin.reshape(shape)
    fine_cos, fine_sin = fine_cos[None, :, None], fine_sin[None, :, None]
    return (coarse_cos * fine_cos - coarse_sin * fine_sin).reshape(2 * freq_rows, 2 * rows_all)


def col_transform(freq_cols, cols_all, freq_block, first):
    fine = math.gcd(16, cols_all)
    freq = first + steps(freq_block)
    coarse_cos, coarse_sin = tables(steps(cols_all // fine, fine)[:, None] * freq[None, :], freq_cols)
    quarter = steps(2, freq_cols // 4)[:, None, None]
    fine_cos, fine_sin = tables(steps(fine)[None, :, None] * freq[None, None, :] + quarter, freq_cols)
    coarse_cos, coarse_sin = coarse_cos[None, :, None], coarse_sin[None, :, None]
    fine_cos, fine_sin = fine_cos[:, None], fine_sin[:, None]
    return (coarse_cos * fine_cos - coarse_sin * fine_sin).reshape(2, cols_all, freq_block)


def mix(symbol, spectra, rhs_count, seg_count):
    freq_rows, freq_cols, pair_count = symbol.shape
    devices, parts, _, width = spectra[0].shape
    count = len(spectra)
    share = width // freq_cols
    step = math.gcd(ROW_STEP, freq_rows)

    def place(field):
        owner, at = divmod(field, share * count)
        group, at = divmod(at, share)
        return group, owner, slice(at * freq_cols, (at + 1) * freq_cols)

    def body(symbol_ref, *refs):
        in_refs, out_refs, turned = refs[:count], refs[count : 2 * count], refs[2 * count]

        def one(u, carry):
            turned[...] = symbol_ref[u].T
            sums = {}
            for t in range(seg_count):
                column = turned[t * seg_count : (t + 1) * seg_count, :]
                for part in range(parts):
                    for k in range(rhs_count):
                        group, owner, lanes = place(k * seg_count + t)
                        term = column * in_refs[group][owner, part, pl.ds(u, 1), lanes]
                        sums[part, k] = sums[part, k] + term if t else term
            for part in range(parts):
                for k in range(rhs_count):
                    for s in range(seg_count):
                        group, owner, lanes = place(k * seg_count + s)
                        out_refs[group][owner, part, pl.ds(u, 1), lanes] = sums[part, k][s : s + 1, :]
            return carry

        lax.fori_loop(0, step, one, 0)

    block = pl.BlockSpec((devices, parts, step, width), lambda i: (0, 0, i, 0))
    return pl.pallas_call(
        body,
        grid=(freq_rows // step,),
        in_specs=[pl.BlockSpec((step, freq_cols, pair_count), lambda i: (i, 0, 0))] + [block] * count,
        out_specs=[block] * count,
        out_shape=[jax.ShapeDtypeStruct(spectra[0].shape, jnp.float32)] * count,
        scratch_shapes=[pltpu.VMEM((pair_count, freq_cols), jnp.float32)],
        name="mix",
    )(symbol, *spectra)


def local(right_side, symbol):
    row_count = lax.axis_size("row")
    col_count = lax.axis_size("col")
    rhs_count, seg_count, row_block, col_block = right_side.shape
    freq_block, freq_width = symbol.shape[:2]
    rows_all = row_block * row_count
    cols_all = col_block * col_count
    freq_rows = freq_block * col_count
    freq_cols = freq_width * row_count
    fields = rhs_count * seg_count
    held = fields // col_count
    to_rows = row_transform(freq_rows, rows_all, freq_block)
    to_cols = col_transform(freq_cols, cols_all, freq_width, lax.axis_index("row") * freq_width)
    count = math.gcd(2, held)
    share = held // count
    norm_factor = 1.0 / (freq_rows * freq_cols)
    flat = right_side.reshape(fields, row_block, col_block)
    whole_cols = lax.all_to_all(flat, "col", split_axis=0, concat_axis=2, tiled=True)
    spectra = []
    for group in range(count):
        own = whole_cols[group * share : (group + 1) * share]
        whole = lax.all_gather(own, "row", axis=1, tiled=True)
        half = jnp.einsum("prc,zcv->zrpv", whole, to_cols, precision=PRECISION)
        half = half.reshape(2 * rows_all, share * freq_width)
        spectrum = jnp.dot(to_rows, half, precision=PRECISION)
        spectrum = spectrum.reshape(col_count, 2, freq_block, share * freq_width)
        spectra.append(lax.all_to_all(spectrum, "col", split_axis=0, concat_axis=0, tiled=True))
    mixtures = mix(symbol, spectra, rhs_count, seg_count)
    sums = []
    for spectrum, mixed in zip(spectra, mixtures):
        for at in range(share):
            lanes = slice(at * freq_width, (at + 1) * freq_width)
            sums.append(jnp.sum(spectrum[..., lanes] * mixed[..., lanes], axis=(1, 2, 3)))
    curve = jnp.stack(sums, axis=1).reshape(rhs_count, seg_count).sum(axis=1) * norm_factor
    norm_now = jnp.sum(right_side * right_side, axis=(1, 2, 3))
    norm_now, curve = lax.psum((norm_now, curve), ("row", "col"))
    images = []
    for mixed in mixtures:
        mixed = lax.all_to_all(mixed, "col", split_axis=0, concat_axis=0, tiled=True)
        mixed, norm_now, curve = lax.optimization_barrier((mixed, norm_now, curve))
        mixed = mixed.reshape(2 * freq_rows, share * freq_width)
        back = lax.dot_general(to_rows, mixed, (((0,), (0,)), ((), ())), precision=PRECISION)
        back = back.reshape(2, rows_all, share, freq_width)
        image = jnp.einsum("zrpv,zcv->prc", back, to_cols, precision=PRECISION)
        images.append(lax.psum_scatter(image, "row", scatter_dimension=1, tiled=True))
    image = jnp.concatenate(images, axis=0)
    applied = lax.all_to_all(image, "col", split_axis=2, concat_axis=0, tiled=True)
    applied = applied.reshape(right_side.shape) * norm_factor
    step_size = (norm_now / curve)[:, None, None, None]
    return (step_size * right_side, right_side - step_size * applied)


MESH = pl.DeviceIdType.MESH
VMEM_LIMIT = 60 * 1024 * 1024


def split(value):
    high = value.astype(jnp.bfloat16)
    return high, (value - high.astype(jnp.float32)).astype(jnp.bfloat16)


def product(left, right):
    def one(a, b):
        return jnp.dot(a, b, preferred_element_type=jnp.float32)

    return one(left[0], right[0]) + (one(left[1], right[0]) + one(left[0], right[1]))


class Place:
    def __init__(self, line):
        self.line = line
        self.at, self.me = lax.axis_index("row"), lax.axis_index("col")
        bits = (self.me % 2, (self.me // 2) % 2, self.me // 4)
        self.peers = []
        for turn in range(8):
            flips = (turn % 2, (turn // 2) % 2, turn // 4)
            core, x, y = (bit + flip * (1 - 2 * bit) for bit, flip in zip(bits, flips))
            self.peers.append(y * 4 + x * 2 + core)

    def along(self, hops):
        return (self.at + hops) % self.line

    def greet(self):
        barrier = pltpu.get_barrier_semaphore()
        others = [(self.at, peer) for peer in self.peers[1:]]
        others += [(self.along(hops), self.me) for hops in range(1, self.line)]
        for other in others:
            pl.semaphore_signal(barrier, inc=1, device_id=other, device_id_type=MESH)
        pl.semaphore_wait(barrier, len(others))


def rows_of(at, size):
    return pl.ds(pl.multiple_of(at * size, size), size)


def arrived(ref, sem):
    pltpu.make_async_copy(ref, ref, sem).wait()


def send(src, dst, send_sem, recv_sem, row, col):
    return pltpu.make_async_remote_copy(
        src_ref=src, dst_ref=dst, send_sem=send_sem, recv_sem=recv_sem,
        device_id=(row, col), device_id_type=MESH,
    )


TURNS = (6, 2, 4, 7, 3, 5, 1, 0)


def forward_call(packed, fine, coarse, to_cols, line, freq_block, freq_width):
    rhs_count, seg_count, col_block, row_block = packed.shape
    pair = seg_count // 8
    fields = rhs_count * pair
    rows_all, cols_all = row_block * line, col_block * 8

    def body(packed, fine, coarse, to_cols, spec, stage, pix, high, low, half_high, half_low, out,
             in_send, in_recv, up_send, up_recv, down_send, down_recv, out_send, out_recv):
        here = Place(line)
        at = here.at
        here.greet()

        def first(f, turn):
            k, j = f // pair, f % pair
            src = packed.at[k, here.peers[turn] * pair + j]
            dst = stage.at[f, rows_of(here.me, col_block)]
            if turn == 0:
                return pltpu.make_async_copy(src, dst, in_recv.at[f])
            return send(src, dst, in_send.at[f, turn], in_recv.at[f], at, here.peers[turn])

        for f in range(fields):
            for turn in TURNS:
                first(f, turn).start()

        def build(turn, carry):
            cos_c, sin_c = coarse[0, pl.ds(turn, 1), :], coarse[1, pl.ds(turn, 1), :]
            cos_f, sin_f = fine[0], fine[1]
            cos = split(cos_c * cos_f - sin_c * sin_f)
            sin = split(sin_c * cos_f + cos_c * sin_f)
            for part, table in ((0, high), (1, low)):
                table[turn, :freq_block, :rows_all] = cos[part]
                table[turn, :freq_block, rows_all:] = sin[part]
                table[turn, freq_block:, :rows_all] = -sin[part]
                table[turn, freq_block:, rows_all:] = cos[part]
            return carry

        def block(f, owner):
            return pix.at[f, rows_of(owner, row_block)]

        def up(f, hop):
            own = block(f, here.along(line - hop))
            return send(own, own, up_send.at[f, hop], up_recv.at[f, hop], here.along(1), here.me)

        def down(f, hop):
            own = block(f, here.along(hop))
            return send(own, own, down_send.at[f, hop], down_recv.at[f, hop], here.along(line - 1), here.me)

        def up_goes(hop):
            return (at >= hop) & (at < line - 1)

        def down_goes(hop):
            return (at < line - hop) & (at > 0)

        def enter(f):
            arrived(stage.at[f], in_recv.at[f])
            pix[f, rows_of(at, row_block)] = stage[f].T

            @pl.when(up_goes(0))
            def _():
                up(f, 0).start()

            @pl.when(down_goes(0))
            def _():
                down(f, 0).start()

        def relay(f, hop):
            @pl.when(at >= hop)
            def _():
                arrived(block(f, here.along(line - hop)), up_recv.at[f, hop - 1])

            if hop < line - 1:
                @pl.when(up_goes(hop))
                def _():
                    up(f, hop).start()

            @pl.when(at < line - hop)
            def _():
                arrived(block(f, here.along(hop)), down_recv.at[f, hop - 1])

            if hop < line - 1:
                @pl.when(down_goes(hop))
                def _():
                    down(f, hop).start()

        def leave(f, turn):
            k, j = f // pair, f % pair
            src = out.at[f % 2, turn]
            dst = spec.at[k, here.me * pair + j]
            if turn == 0:
                return pltpu.make_async_copy(src, dst, out_send.at[f, 0])
            return send(src, dst, out_send.at[f, turn], out_recv.at[f, turn], at, here.peers[turn])

        def sent(f):
            leave(f, 0).wait()
            for turn in range(1, 8):
                leave(f, turn).wait_send()

        def compute(f):
            half = product(split(pix[f]), (to_cols[0], to_cols[1]))
            for part in range(2):
                rows = slice(part * rows_all, (part + 1) * rows_all)
                half_high[rows, :], half_low[rows, :] = split(half[:, part * freq_width : (part + 1) * freq_width])

            @pl.when(f >= 2)
            def _():
                sent(f - 2)

            right = (half_high[...], half_low[...])
            for turn in TURNS:
                value = product((high[turn], low[turn]), right)
                out[f % 2, turn] = value.reshape(2, freq_block, freq_width)
                leave(f, turn).start()

        enter(0)
        lax.fori_loop(0, 8, build, 0)

        def step(f, carry):
            for hop in range(1, line - 1):
                relay(f, hop)

            @pl.when(f + 1 < fields)
            def _():
                enter(f + 1)

            relay(f, line - 1)
            compute(f)
            return carry

        lax.fori_loop(0, fields, step, 0)
        sent(fields - 2)
        sent(fields - 1)

        def finish(f, carry):
            for turn in range(1, 8):
                first(f, turn).wait_send()
                leave(f, turn).wait_recv()
            for hop in range(line - 1):
                @pl.when(up_goes(hop))
                def _():
                    up(f, hop).wait_send()

                @pl.when(down_goes(hop))
                def _():
                    down(f, hop).wait_send()
            return carry

        lax.fori_loop(0, fields, finish, 0)

    dma = pltpu.SemaphoreType.DMA
    vmem = pl.BlockSpec(memory_space=pltpu.VMEM)
    hbm = pl.BlockSpec(memory_space=pl.ANY)
    hops = dma((fields, line - 1))
    return pl.pallas_call(
        body,
        in_specs=[hbm, vmem, vmem, vmem],
        out_specs=hbm,
        out_shape=jax.ShapeDtypeStruct((rhs_count, seg_count, 2, freq_block, freq_width), jnp.float32),
        scratch_shapes=[
            pltpu.VMEM((fields, cols_all, row_block), jnp.float32),
            pltpu.VMEM((fields, rows_all, cols_all), jnp.float32),
            pltpu.VMEM((8, 2 * freq_block, 2 * rows_all), jnp.bfloat16),
            pltpu.VMEM((8, 2 * freq_block, 2 * rows_all), jnp.bfloat16),
            pltpu.VMEM((2 * rows_all, freq_width), jnp.bfloat16),
            pltpu.VMEM((2 * rows_all, freq_width), jnp.bfloat16),
            pltpu.VMEM((2, 8, 2, freq_block, freq_width), jnp.float32),
            dma((fields, 8)), dma((fields,)), hops, hops, hops, hops, dma((fields, 8)), dma((fields, 8)),
        ],
        compiler_params=pltpu.CompilerParams(
            collective_id=0, has_side_effects=True, vmem_limit_bytes=VMEM_LIMIT
        ),
        name="forward",
    )(packed, fine, coarse, to_cols)


def backward_call(mixed, scalars, fine, coarse, from_cols, line, row_block, col_block):
    rhs_count, seg_count, _, freq_block, freq_width = mixed.shape
    pair = seg_count // 8
    fields = rhs_count * pair
    rows_all, cols_all = row_block * line, col_block * 8

    def body(mixed, scalars, fine, coarse, from_cols, image, totals, got, part_sum, high, low,
             half_high, half_low, up_in, down_in, turned, line_sums, line_total, plane_sums,
             in_send, in_recv, up_send, up_recv, down_send, down_recv, out_send, out_recv,
             line_send, line_recv, plane_send, plane_recv):
        here = Place(line)
        at = here.at
        here.greet()

        def enter(f, turn):
            k, j = f // pair, f % pair
            src, dst = mixed.at[k, here.peers[turn] * pair + j], got.at[f, turn]
            if turn == 0:
                return pltpu.make_async_copy(src, dst, in_recv.at[f, 0])
            return send(src, dst, in_send.at[f, turn], in_recv.at[f, turn], at, here.peers[turn])

        def along_line(hops):
            return send(scalars, line_sums.at[hops], line_send.at[hops], line_recv.at[hops],
                        here.along(hops), here.me)

        def in_plane(turn):
            return send(line_total, plane_sums.at[turn], plane_send.at[turn], plane_recv.at[turn],
                        at, here.peers[turn])

        for hops in range(1, line):
            along_line(hops).start()

        def begin(f, carry):
            for turn in TURNS:
                enter(f, turn).start()
            return carry

        lax.fori_loop(0, fields, begin, 0)

        def build(turn, carry):
            cos_f, sin_f = fine[0], fine[1]
            cos_c, sin_c = coarse[0, turn], coarse[1, turn]
            cos = split(cos_c * cos_f - sin_c * sin_f)
            sin = split(sin_c * cos_f + cos_c * sin_f)
            for part, table in ((0, high), (1, low)):
                for half in range(2):
                    lanes = rows_of(turn * 2 + half, freq_block)
                    table[:rows_all, lanes] = -sin[part] if half else cos[part]
                    table[rows_all:, lanes] = cos[part] if half else sin[part]
            return carry

        lax.fori_loop(0, 8, build, 0)
        total = scalars[...]
        for hops in range(1, line):
            along_line(hops).wait()
            total = total + line_sums[hops]
        line_total[...] = total

        def block(f, owner):
            return part_sum.at[f, rows_of(owner, row_block)]

        def up(f, owner):
            return send(block(f, owner), up_in.at[f, owner - 1], up_send.at[f, owner - 1],
                        up_recv.at[f, owner - 1], here.along(1), here.me)

        def down(f, owner):
            return send(block(f, owner), down_in.at[f, owner], down_send.at[f, owner],
                        down_recv.at[f, owner], here.along(line - 1), here.me)

        def add(f, owner, extra):
            rows = rows_of(owner, row_block)
            part_sum[f, rows] = part_sum[f, rows] + extra

        def up_add(f, owner):
            arrived(up_in.at[f, owner - 1], up_recv.at[f, owner - 1])
            add(f, owner, up_in[f, owner - 1])

        def down_add(f, owner):
            arrived(down_in.at[f, owner], down_recv.at[f, owner])
            add(f, owner, down_in[f, owner])

        def compute(f):
            for turn in range(8):
                arrived(got.at[f, turn], in_recv.at[f, turn])
            spectrum = split(got[f].reshape(16 * freq_block, freq_width))
            half = product((high[...], low[...]), spectrum)
            for part in range(2):
                lanes = slice(part * freq_width, (part + 1) * freq_width)
                half_high[:, lanes], half_low[:, lanes] = split(half[part * rows_all : (part + 1) * rows_all])
            part_sum[f] = product((half_high[...], half_low[...]), (from_cols[0], from_cols[1]))

        def relay(f, hop):
            high_end, low_end = line - hop, hop - 1

            @pl.when((at > 0) & (at < high_end))
            def _():
                up_add(f, high_end)

            @pl.when(at < high_end)
            def _():
                up(f, high_end).start()

            @pl.when((at < line - 1) & (at > low_end))
            def _():
                down_add(f, low_end)

            @pl.when(at > low_end)
            def _():
                down(f, low_end).start()

        def leave(f, turn):
            k, j = f // pair, f % pair
            src = turned.at[f, rows_of(here.peers[turn], col_block)]
            dst = image.at[k, here.me * pair + j]
            if turn == 0:
                return pltpu.make_async_copy(src, dst, out_send.at[f, 0])
            return send(src, dst, out_send.at[f, turn], out_recv.at[f, turn], at, here.peers[turn])

        def final(f):
            @pl.when(at > 0)
            def _():
                up_add(f, at)

            @pl.when(at < line - 1)
            def _():
                down_add(f, at)

            turned[f] = part_sum[f, rows_of(at, row_block)].T
            for turn in TURNS:
                leave(f, turn).start()

        for turn in range(1, 8):
            in_plane(turn).start()

        def step(f, carry):
            @pl.when(f < fields)
            def _():
                compute(f)
                relay(f, 1)

            @pl.when(f > 0)
            def _():
                final(f - 1)

            @pl.when(f < fields)
            def _():
                for hop in range(2, line):
                    relay(f, hop)

            return carry

        lax.fori_loop(0, fields + 1, step, 0)
        total = line_total[...]
        for turn in range(1, 8):
            in_plane(turn).wait()
            total = total + plane_sums[turn]
        totals[...] = total

        def finish(f, carry):
            leave(f, 0).wait()
            for turn in range(1, 8):
                enter(f, turn).wait_send()
                leave(f, turn).wait()
            for owner in range(line):
                if owner > 0:
                    @pl.when(at < owner)
                    def _():
                        up(f, owner).wait_send()

                if owner < line - 1:
                    @pl.when(at > owner)
                    def _():
                        down(f, owner).wait_send()
            return carry

        lax.fori_loop(0, fields, finish, 0)

    dma = pltpu.SemaphoreType.DMA
    vmem = pl.BlockSpec(memory_space=pltpu.VMEM)
    hbm = pl.BlockSpec(memory_space=pl.ANY)
    hops = dma((fields, line - 1))
    stream = pltpu.VMEM((fields, line - 1, row_block, cols_all), jnp.float32)
    return pl.pallas_call(
        body,
        in_specs=[hbm, vmem, vmem, vmem, vmem],
        out_specs=[hbm, vmem],
        out_shape=[
            jax.ShapeDtypeStruct((rhs_count, seg_count, col_block, row_block), jnp.float32),
            jax.ShapeDtypeStruct(scalars.shape, jnp.float32),
        ],
        scratch_shapes=[
            pltpu.VMEM((fields, 8, 2, freq_block, freq_width), jnp.float32),
            pltpu.VMEM((fields, rows_all, cols_all), jnp.float32),
            pltpu.VMEM((2 * rows_all, 16 * freq_block), jnp.bfloat16),
            pltpu.VMEM((2 * rows_all, 16 * freq_block), jnp.bfloat16),
            pltpu.VMEM((rows_all, 2 * freq_width), jnp.bfloat16),
            pltpu.VMEM((rows_all, 2 * freq_width), jnp.bfloat16),
            stream, stream,
            pltpu.VMEM((fields, cols_all, row_block), jnp.float32),
            pltpu.VMEM((line,) + scalars.shape, jnp.float32),
            pltpu.VMEM(scalars.shape, jnp.float32),
            pltpu.VMEM((8,) + scalars.shape, jnp.float32),
            dma((fields, 8)), dma((fields, 8)), hops, hops, hops, hops, dma((fields, 8)), dma((fields, 8)),
            dma((line,)), dma((line,)), dma((8,)), dma((8,)),
        ],
        compiler_params=pltpu.CompilerParams(
            collective_id=1, has_side_effects=True, vmem_limit_bytes=VMEM_LIMIT
        ),
        name="backward",
    )(mixed, scalars, fine, coarse, from_cols)


def mix_all(symbol, spectra):
    freq_rows, freq_cols, pair_count = symbol.shape
    rhs_count, seg_count, parts = spectra.shape[:3]
    step = math.gcd(ROW_STEP, freq_rows)

    def body(symbol_ref, in_ref, out_ref, curve_ref, turned):
        def one(u, carry):
            turned[...] = symbol_ref[u].T
            sums = {}
            for t in range(seg_count):
                column = turned[t * seg_count : (t + 1) * seg_count, :]
                for part in range(parts):
                    for k in range(rhs_count):
                        term = column * in_ref[k, t, part, pl.ds(u, 1), :]
                        sums[part, k] = sums[part, k] + term if t else term
            for part in range(parts):
                for k in range(rhs_count):
                    for s in range(seg_count):
                        out_ref[k, s, part, pl.ds(u, 1), :] = sums[part, k][s : s + 1, :]
            return carry

        lax.fori_loop(0, step, one, 0)

        @pl.when(pl.program_id(0) == 0)
        def _():
            curve_ref[...] = jnp.zeros_like(curve_ref)

        for k in range(rhs_count):
            total = curve_ref[k]
            for t in range(seg_count):
                for part in range(parts):
                    total = total + in_ref[k, t, part] * out_ref[k, t, part]
            curve_ref[k] = total

    block = pl.BlockSpec((rhs_count, seg_count, parts, step, freq_cols), lambda i: (0, 0, 0, i, 0))
    return pl.pallas_call(
        body,
        grid=(freq_rows // step,),
        in_specs=[pl.BlockSpec((step, freq_cols, pair_count), lambda i: (i, 0, 0)), block],
        out_specs=[block, pl.BlockSpec((rhs_count, step, freq_cols), lambda i: (0, 0, 0))],
        out_shape=[
            jax.ShapeDtypeStruct(spectra.shape, jnp.float32),
            jax.ShapeDtypeStruct((rhs_count, step, freq_cols), jnp.float32),
        ],
        scratch_shapes=[pltpu.VMEM((pair_count, freq_cols), jnp.float32)],
        name="mix",
    )(symbol, spectra)


def halves(table):
    high = lax.reduce_precision(table, 8, 7)
    return jnp.stack([high, table - high]).astype(jnp.bfloat16)


def routed(right_side, symbol):
    line = lax.axis_size("row")
    rhs_count, seg_count, row_block, col_block = right_side.shape
    freq_block, freq_width = symbol.shape[:2]
    rows_all, cols_all = row_block * line, col_block * 8
    freq_rows, freq_cols = freq_block * 8, freq_width * line
    norm_factor = 1.0 / (freq_rows * freq_cols)
    owners = jnp.stack(Place(line).peers)
    fine = jnp.stack(tables(steps(freq_block)[:, None] * steps(rows_all)[None, :], freq_rows))
    coarse = jnp.stack(tables(owners[:, None] * steps(rows_all, freq_block)[None, :], freq_rows))
    to_cols = col_transform(freq_cols, cols_all, freq_width, lax.axis_index("row") * freq_width)
    norm_now = jnp.sum(right_side * right_side, axis=(1, 2, 3))
    spectra = forward_call(
        right_side.transpose(0, 1, 3, 2), fine, coarse,
        halves(to_cols.transpose(1, 0, 2).reshape(cols_all, 2 * freq_width)), line, freq_block, freq_width,
    )
    mixed, curve = mix_all(symbol, spectra)
    curve = jnp.sum(curve, axis=(1, 2)) * norm_factor
    scalars = jnp.broadcast_to(jnp.stack([norm_now, curve])[..., None], (2, rhs_count, 128))
    image, totals = backward_call(
        mixed, scalars, fine.transpose(0, 2, 1), coarse[..., None],
        halves(to_cols.transpose(0, 2, 1).reshape(2 * freq_width, cols_all)), line, row_block, col_block,
    )
    applied = image.transpose(0, 1, 3, 2) * norm_factor
    step_size = (totals[0, :, 0] / totals[1, :, 0])[:, None, None, None]
    return (step_size * right_side, right_side - step_size * applied)


def fits(mesh, right_side, symbol):
    ring, wide = mesh.shape["row"], mesh.shape["col"]
    _, seg_count, rows, cols = right_side.shape
    freq_rows, freq_cols = symbol.shape[:2]
    aligned = all(n % 128 == 0 for n in (rows // ring, freq_rows // wide, freq_cols // ring))
    return ring > 1 and wide == 8 and seg_count % 8 == 0 and cols // wide % 8 == 0 and aligned


def solution(mesh):
    placed = P(None, None, "row", "col")

    def whole(right_side, symbol):
        return jax.shard_map(
            routed if fits(mesh, right_side, symbol) else local,
            mesh=mesh,
            in_specs=(placed, P("col", "row", None)),
            out_specs=(placed, placed),
            check_vma=False,
        )(right_side, symbol)

    return whole
```

```python
import math

import jax
import jax.numpy as jnp
from jax import lax
from jax.experimental import pallas as pl
from jax.experimental.pallas import tpu as pltpu
from jax.sharding import PartitionSpec as P

PRECISION = lax.Precision.HIGH
ROW_STEP = 8


def tables(phase, length):
    angle = (phase % length).astype(jnp.float32) * (2.0 * math.pi / length)
    return lax.optimization_barrier((jnp.cos(angle), jnp.sin(angle)))


def steps(count, stride=1):
    return jnp.arange(count, dtype=jnp.int32) * stride


def row_transform(freq_rows, rows_all, freq_block):
    fine = math.gcd(32, freq_block)
    place = jnp.tile(steps(rows_all), 2)
    part_in = jnp.repeat(steps(2), rows_all)
    coarse_cos, coarse_sin = tables(steps(freq_rows // fine, fine)[:, None] * place[None, :], freq_rows)
    quarter = (steps(2)[:, None] - part_in[None, :]) * (freq_rows // 4) + freq_rows
    fine_cos, fine_sin = tables(
        steps(fine)[None, :, None] * place[None, None, :] + quarter[:, None, :], freq_rows
    )
    shape = (freq_rows // freq_block, 1, freq_block // fine, 1, 2 * rows_all)
    coarse_cos, coarse_sin = coarse_cos.reshape(shape), coarse_sin.reshape(shape)
    fine_cos, fine_sin = fine_cos[None, :, None], fine_sin[None, :, None]
    return (coarse_cos * fine_cos - coarse_sin * fine_sin).reshape(2 * freq_rows, 2 * rows_all)


def col_transform(freq_cols, cols_all, freq_block, first):
    fine = math.gcd(16, cols_all)
    freq = first + steps(freq_block)
    coarse_cos, coarse_sin = tables(steps(cols_all // fine, fine)[:, None] * freq[None, :], freq_cols)
    quarter = steps(2, freq_cols // 4)[:, None, None]
    fine_cos, fine_sin = tables(steps(fine)[None, :, None] * freq[None, None, :] + quarter, freq_cols)
    coarse_cos, coarse_sin = coarse_cos[None, :, None], coarse_sin[None, :, None]
    fine_cos, fine_sin = fine_cos[:, None], fine_sin[:, None]
    return (coarse_cos * fine_cos - coarse_sin * fine_sin).reshape(2, cols_all, freq_block)


def mix(symbol, spectra, rhs_count, seg_count):
    freq_rows, freq_cols, pair_count = symbol.shape
    devices, parts, _, width = spectra[0].shape
    count = len(spectra)
    share = width // freq_cols
    step = math.gcd(ROW_STEP, freq_rows)

    def place(field):
        owner, at = divmod(field, share * count)
        group, at = divmod(at, share)
        return group, owner, slice(at * freq_cols, (at + 1) * freq_cols)

    def body(symbol_ref, *refs):
        in_refs, out_refs, turned = refs[:count], refs[count : 2 * count], refs[2 * count]

        def one(u, carry):
            turned[...] = symbol_ref[u].T
            sums = {}
            for t in range(seg_count):
                column = turned[t * seg_count : (t + 1) * seg_count, :]
                for part in range(parts):
                    for k in range(rhs_count):
                        group, owner, lanes = place(k * seg_count + t)
                        term = column * in_refs[group][owner, part, pl.ds(u, 1), lanes]
                        sums[part, k] = sums[part, k] + term if t else term
            for part in range(parts):
                for k in range(rhs_count):
                    for s in range(seg_count):
                        group, owner, lanes = place(k * seg_count + s)
                        out_refs[group][owner, part, pl.ds(u, 1), lanes] = sums[part, k][s : s + 1, :]
            return carry

        lax.fori_loop(0, step, one, 0)

    block = pl.BlockSpec((devices, parts, step, width), lambda i: (0, 0, i, 0))
    return pl.pallas_call(
        body,
        grid=(freq_rows // step,),
        in_specs=[pl.BlockSpec((step, freq_cols, pair_count), lambda i: (i, 0, 0))] + [block] * count,
        out_specs=[block] * count,
        out_shape=[jax.ShapeDtypeStruct(spectra[0].shape, jnp.float32)] * count,
        scratch_shapes=[pltpu.VMEM((pair_count, freq_cols), jnp.float32)],
        name="mix",
    )(symbol, *spectra)


def local(right_side, symbol):
    row_count = lax.axis_size("row")
    col_count = lax.axis_size("col")
    rhs_count, seg_count, row_block, col_block = right_side.shape
    freq_block, freq_width = symbol.shape[:2]
    rows_all = row_block * row_count
    cols_all = col_block * col_count
    freq_rows = freq_block * col_count
    freq_cols = freq_width * row_count
    fields = rhs_count * seg_count
    held = fields // col_count
    to_rows = row_transform(freq_rows, rows_all, freq_block)
    to_cols = col_transform(freq_cols, cols_all, freq_width, lax.axis_index("row") * freq_width)
    count = math.gcd(2, held)
    share = held // count
    norm_factor = 1.0 / (freq_rows * freq_cols)
    flat = right_side.reshape(fields, row_block, col_block)
    whole_cols = lax.all_to_all(flat, "col", split_axis=0, concat_axis=2, tiled=True)
    spectra = []
    for group in range(count):
        own = whole_cols[group * share : (group + 1) * share]
        whole = lax.all_gather(own, "row", axis=1, tiled=True)
        half = jnp.einsum("prc,zcv->zrpv", whole, to_cols, precision=PRECISION)
        half = half.reshape(2 * rows_all, share * freq_width)
        spectrum = jnp.dot(to_rows, half, precision=PRECISION)
        spectrum = spectrum.reshape(col_count, 2, freq_block, share * freq_width)
        spectra.append(lax.all_to_all(spectrum, "col", split_axis=0, concat_axis=0, tiled=True))
    mixtures = mix(symbol, spectra, rhs_count, seg_count)
    sums = []
    for spectrum, mixed in zip(spectra, mixtures):
        for at in range(share):
            lanes = slice(at * freq_width, (at + 1) * freq_width)
            sums.append(jnp.sum(spectrum[..., lanes] * mixed[..., lanes], axis=(1, 2, 3)))
    curve = jnp.stack(sums, axis=1).reshape(rhs_count, seg_count).sum(axis=1) * norm_factor
    norm_now = jnp.sum(right_side * right_side, axis=(1, 2, 3))
    norm_now, curve = lax.psum((norm_now, curve), ("row", "col"))
    images = []
    for mixed in mixtures:
        mixed = lax.all_to_all(mixed, "col", split_axis=0, concat_axis=0, tiled=True)
        mixed, norm_now, curve = lax.optimization_barrier((mixed, norm_now, curve))
        mixed = mixed.reshape(2 * freq_rows, share * freq_width)
        back = lax.dot_general(to_rows, mixed, (((0,), (0,)), ((), ())), precision=PRECISION)
        back = back.reshape(2, rows_all, share, freq_width)
        image = jnp.einsum("zrpv,zcv->prc", back, to_cols, precision=PRECISION)
        images.append(lax.psum_scatter(image, "row", scatter_dimension=1, tiled=True))
    image = jnp.concatenate(images, axis=0)
    applied = lax.all_to_all(image, "col", split_axis=2, concat_axis=0, tiled=True)
    applied = applied.reshape(right_side.shape) * norm_factor
    step_size = (norm_now / curve)[:, None, None, None]
    return (step_size * right_side, right_side - step_size * applied)


MESH = pl.DeviceIdType.MESH
VMEM_LIMIT = 60 * 1024 * 1024


def split(value):
    high = value.astype(jnp.bfloat16)
    return high, (value - high.astype(jnp.float32)).astype(jnp.bfloat16)


def product(left, right):
    def one(a, b):
        return jnp.dot(a, b, preferred_element_type=jnp.float32)

    return one(left[0], right[0]) + (one(left[1], right[0]) + one(left[0], right[1]))


def product_across(left, right):
    def one(a, b):
        return lax.dot_general(a, b, (((1,), (1,)), ((), ())), preferred_element_type=jnp.float32)

    return one(left[0], right[0]) + (one(left[1], right[0]) + one(left[0], right[1]))


def mix_scratch(symbol, seg_count, step):
    freq_rows, freq_cols, pair_count = symbol.shape
    block = pltpu.VMEM((2, seg_count, 2, step, freq_cols), jnp.float32)
    dma = pltpu.SemaphoreType.DMA
    return [
        pltpu.VMEM((2, step, freq_cols, pair_count), jnp.float32), block, block,
        pltpu.VMEM((pair_count, freq_cols), jnp.float32),
        dma((2,)), dma((2,)), dma((2,)),
    ]


def mix_one(symbol, spectra, mixed, curve, scratch):
    symbols, ins, outs, turned, symbol_sem, in_sem, out_sem = scratch
    seg_count, parts, freq_rows, _ = spectra.shape
    step = symbols.shape[1]
    count = freq_rows // step

    def load(c):
        rows, slot = rows_of(c, step), c % 2
        pltpu.make_async_copy(symbol.at[rows], symbols.at[slot], symbol_sem.at[slot]).start()
        pltpu.make_async_copy(spectra.at[:, :, rows], ins.at[slot], in_sem.at[slot]).start()

    def store(c):
        slot = c % 2
        return pltpu.make_async_copy(outs.at[slot], mixed.at[:, :, rows_of(c, step)], out_sem.at[slot])

    load(0)
    curve[...] = jnp.zeros_like(curve)

    def chunk(c, carry):
        slot = c % 2

        @pl.when(c + 1 < count)
        def _():
            load(c + 1)

        arrived(symbols.at[slot], symbol_sem.at[slot])
        arrived(ins.at[slot], in_sem.at[slot])

        @pl.when(c >= 2)
        def _():
            store(c - 2).wait()

        def one(u, inner):
            turned[...] = symbols[slot, u].T
            sums = [None] * parts
            for t in range(seg_count):
                column = turned[t * seg_count : (t + 1) * seg_count, :]
                for part in range(parts):
                    term = column * ins[slot, t, part, pl.ds(u, 1), :]
                    sums[part] = sums[part] + term if t else term
            for part in range(parts):
                for t in range(seg_count):
                    outs[slot, t, part, pl.ds(u, 1), :] = sums[part][t : t + 1, :]
            return inner

        lax.fori_loop(0, step, one, 0)
        total = curve[...]
        for t in range(seg_count):
            for part in range(parts):
                total = total + ins[slot, t, part] * outs[slot, t, part]
        curve[...] = total
        store(c).start()
        return carry

    lax.fori_loop(0, count, chunk, 0)
    store(count - 2).wait()
    store(count - 1).wait()


class Place:
    def __init__(self, line):
        self.line = line
        self.at, self.me = lax.axis_index("row"), lax.axis_index("col")
        bits = (self.me % 2, (self.me // 2) % 2, self.me // 4)
        self.peers = []
        for turn in range(8):
            flips = (turn % 2, (turn // 2) % 2, turn // 4)
            core, x, y = (bit + flip * (1 - 2 * bit) for bit, flip in zip(bits, flips))
            self.peers.append(y * 4 + x * 2 + core)

    def along(self, hops):
        return (self.at + hops) % self.line

    def greet(self):
        barrier = pltpu.get_barrier_semaphore()
        others = [(self.at, peer) for peer in self.peers[1:]]
        others += [(self.along(hops), self.me) for hops in range(1, self.line)]
        for other in others:
            pl.semaphore_signal(barrier, inc=1, device_id=other, device_id_type=MESH)
        pl.semaphore_wait(barrier, len(others))


def rows_of(at, size):
    return pl.ds(pl.multiple_of(at * size, size), size)


def arrived(ref, sem):
    pltpu.make_async_copy(ref, ref, sem).wait()


def send(src, dst, send_sem, recv_sem, row, col):
    return pltpu.make_async_remote_copy(
        src_ref=src, dst_ref=dst, send_sem=send_sem, recv_sem=recv_sem,
        device_id=(row, col), device_id_type=MESH,
    )


TURNS = (6, 2, 4, 7, 3, 5, 1, 0)


def forward_call(packed, symbol, fine, coarse, to_cols, line):
    freq_block, freq_width = symbol.shape[:2]
    mix_step = math.gcd(ROW_STEP, freq_block)
    rhs_count, seg_count, col_block, row_block = packed.shape
    pair = seg_count // 8
    fields = rhs_count * pair
    rows_all, cols_all = row_block * line, col_block * 8

    def body(packed, symbol, fine, coarse, to_cols, spec, mixed, curve, stage, pix, high, low, half_high, half_low, out,
             in_send, in_recv, up_send, up_recv, down_send, down_recv, out_send, out_recv, *mix_refs):
        here = Place(line)
        at = here.at
        here.greet()

        def first(f, turn):
            k, j = f // pair, f % pair
            src = packed.at[k, here.peers[turn] * pair + j]
            dst = stage.at[f, rows_of(here.me, col_block)]
            if turn == 0:
                return pltpu.make_async_copy(src, dst, in_recv.at[f])
            return send(src, dst, in_send.at[f, turn], in_recv.at[f], at, here.peers[turn])

        for f in range(fields):
            for turn in TURNS:
                first(f, turn).start()

        def build(turn, carry):
            cos_c, sin_c = coarse[0, pl.ds(turn, 1), :], coarse[1, pl.ds(turn, 1), :]
            cos_f, sin_f = fine[0], fine[1]
            cos = split(cos_c * cos_f - sin_c * sin_f)
            sin = split(sin_c * cos_f + cos_c * sin_f)
            for part, table in ((0, high), (1, low)):
                table[turn, :freq_block, :rows_all] = cos[part]
                table[turn, :freq_block, rows_all:] = sin[part]
                table[turn, freq_block:, :rows_all] = -sin[part]
                table[turn, freq_block:, rows_all:] = cos[part]
            return carry

        def block(f, owner):
            return pix.at[f, rows_of(owner, row_block)]

        def up(f, hop):
            own = block(f, here.along(line - hop))
            return send(own, own, up_send.at[f, hop], up_recv.at[f, hop], here.along(1), here.me)

        def down(f, hop):
            own = block(f, here.along(hop))
            return send(own, own, down_send.at[f, hop], down_recv.at[f, hop], here.along(line - 1), here.me)

        def up_goes(hop):
            return (at >= hop) & (at < line - 1)

        def down_goes(hop):
            return (at < line - hop) & (at > 0)

        def enter(f):
            arrived(stage.at[f], in_recv.at[f])
            pix[f, rows_of(at, row_block)] = stage[f].T

            @pl.when(up_goes(0))
            def _():
                up(f, 0).start()

            @pl.when(down_goes(0))
            def _():
                down(f, 0).start()

        def relay(f, hop):
            @pl.when(at >= hop)
            def _():
                arrived(block(f, here.along(line - hop)), up_recv.at[f, hop - 1])

            if hop < line - 1:
                @pl.when(up_goes(hop))
                def _():
                    up(f, hop).start()

            @pl.when(at < line - hop)
            def _():
                arrived(block(f, here.along(hop)), down_recv.at[f, hop - 1])

            if hop < line - 1:
                @pl.when(down_goes(hop))
                def _():
                    down(f, hop).start()

        def leave(f, turn):
            k, j = f // pair, f % pair
            src = out.at[f % 2, turn]
            dst = spec.at[k, here.me * pair + j]
            if turn == 0:
                return pltpu.make_async_copy(src, dst, out_send.at[f, 0])
            return send(src, dst, out_send.at[f, turn], out_recv.at[f, turn], at, here.peers[turn])

        def sent(f):
            leave(f, 0).wait()
            for turn in range(1, 8):
                leave(f, turn).wait_send()

        def compute(f):
            half = product(split(pix[f]), (to_cols[0], to_cols[1]))
            for part in range(2):
                rows = slice(part * rows_all, (part + 1) * rows_all)
                half_high[rows, :], half_low[rows, :] = split(half[:, part * freq_width : (part + 1) * freq_width])

            @pl.when(f >= 2)
            def _():
                sent(f - 2)

            right = (half_high[...], half_low[...])
            for turn in TURNS:
                value = product((high[turn], low[turn]), right)
                out[f % 2, turn] = value.reshape(2, freq_block, freq_width)
                leave(f, turn).start()

        enter(0)
        lax.fori_loop(0, 8, build, 0)

        def step(f, carry):
            for hop in range(1, line - 1):
                relay(f, hop)

            @pl.when(f + 1 < fields)
            def _():
                enter(f + 1)

            relay(f, line - 1)
            compute(f)
            return carry

        lax.fori_loop(0, fields, step, 0)

        def landed(f, carry):
            for turn in range(1, 8):
                leave(f, turn).wait_recv()
            return carry

        lax.fori_loop(0, pair, landed, 0)
        mix_one(symbol, spec.at[0], mixed, curve, mix_refs)
        lax.fori_loop(pair, fields, landed, 0)
        sent(fields - 2)
        sent(fields - 1)

        def finish(f, carry):
            for turn in range(1, 8):
                first(f, turn).wait_send()
            for hop in range(line - 1):
                @pl.when(up_goes(hop))
                def _():
                    up(f, hop).wait_send()

                @pl.when(down_goes(hop))
                def _():
                    down(f, hop).wait_send()
            return carry

        lax.fori_loop(0, fields, finish, 0)

    dma = pltpu.SemaphoreType.DMA
    vmem = pl.BlockSpec(memory_space=pltpu.VMEM)
    hbm = pl.BlockSpec(memory_space=pl.ANY)
    hops = dma((fields, line - 1))
    return pl.pallas_call(
        body,
        in_specs=[hbm, hbm, vmem, vmem, vmem],
        out_specs=[hbm, hbm, vmem],
        out_shape=[
            jax.ShapeDtypeStruct((rhs_count, seg_count, 2, freq_block, freq_width), jnp.float32),
            jax.ShapeDtypeStruct((seg_count, 2, freq_block, freq_width), jnp.float32),
            jax.ShapeDtypeStruct((mix_step, freq_width), jnp.float32),
        ],
        scratch_shapes=[
            pltpu.VMEM((fields, cols_all, row_block), jnp.float32),
            pltpu.VMEM((fields, rows_all, cols_all), jnp.float32),
            pltpu.VMEM((8, 2 * freq_block, 2 * rows_all), jnp.bfloat16),
            pltpu.VMEM((8, 2 * freq_block, 2 * rows_all), jnp.bfloat16),
            pltpu.VMEM((2 * rows_all, freq_width), jnp.bfloat16),
            pltpu.VMEM((2 * rows_all, freq_width), jnp.bfloat16),
            pltpu.VMEM((2, 8, 2, freq_block, freq_width), jnp.float32),
            dma((fields, 8)), dma((fields,)), hops, hops, hops, hops, dma((fields, 8)), dma((fields, 8)),
        ] + mix_scratch(symbol, seg_count, mix_step),
        compiler_params=pltpu.CompilerParams(
            collective_id=0, has_side_effects=True, vmem_limit_bytes=VMEM_LIMIT
        ),
        name="forward",
    )(packed, symbol, fine, coarse, to_cols)


def backward_call(symbol, spectra, mixed, norms, curve, fine, coarse, to_cols, line, row_block, col_block):
    rhs_count, seg_count, _, freq_block, freq_width = spectra.shape
    mix_step = curve.shape[0]
    sums_shape = (2,) + norms.shape
    pair = seg_count // 8
    fields = rhs_count * pair
    rows_all, cols_all = row_block * line, col_block * 8

    def body(symbol, spectra, mixed, norms, curve, fine, coarse, to_cols, image, totals, mixed_last,
             got, part_sum, high, low,
             half_high, half_low, up_in, down_in, turned, scalars, line_sums, line_total, plane_sums, curve_last,
             in_send, in_recv, up_send, up_recv, down_send, down_recv, out_send, out_recv,
             line_send, line_recv, plane_send, plane_recv, *mix_refs):
        here = Place(line)
        at = here.at
        here.greet()

        def enter(last, j, turn):
            f = last * pair + j
            src = (mixed_last if last else mixed).at[here.peers[turn] * pair + j]
            dst = got.at[f, turn]
            if turn == 0:
                return pltpu.make_async_copy(src, dst, in_recv.at[f, 0])
            return send(src, dst, in_send.at[f, turn], in_recv.at[f, turn], at, here.peers[turn])

        def along_line(hops):
            return send(scalars, line_sums.at[hops], line_send.at[hops], line_recv.at[hops],
                        here.along(hops), here.me)

        def in_plane(turn):
            return send(line_total, plane_sums.at[turn], plane_send.at[turn], plane_recv.at[turn],
                        at, here.peers[turn])

        def begin(last):
            for j in range(pair):
                for turn in TURNS:
                    enter(last, j, turn).start()

        begin(0)

        def build(turn, carry):
            cos_c, sin_c = coarse[0, pl.ds(turn, 1), :], coarse[1, pl.ds(turn, 1), :]
            cos_f, sin_f = fine[0], fine[1]
            cos = split((cos_c * cos_f - sin_c * sin_f).T)
            sin = split((sin_c * cos_f + cos_c * sin_f).T)
            for part, table in ((0, high), (1, low)):
                for half in range(2):
                    lanes = rows_of(turn * 2 + half, freq_block)
                    table[:rows_all, lanes] = -sin[part] if half else cos[part]
                    table[rows_all:, lanes] = cos[part] if half else sin[part]
            return carry

        mix_one(symbol, spectra.at[rhs_count - 1], mixed_last, curve_last, mix_refs)
        begin(1)
        scalars[0] = norms[...]
        for k, part in ((0, curve), (1, curve_last)):
            whole = jnp.sum(jnp.sum(part[...], axis=0, keepdims=True), axis=1, keepdims=True)
            scalars[1, k : k + 1, :] = jnp.broadcast_to(whole, (1, norms.shape[1]))
        lax.fori_loop(0, 8, build, 0)
        for hops in range(1, line):
            along_line(hops).start()
        total = scalars[...]
        for hops in range(1, line):
            along_line(hops).wait()
            total = total + line_sums[hops]
        line_total[...] = total

        def block(f, owner):
            return part_sum.at[f, rows_of(owner, row_block)]

        def up(f, owner):
            return send(block(f, owner), up_in.at[f, owner - 1], up_send.at[f, owner - 1],
                        up_recv.at[f, owner - 1], here.along(1), here.me)

        def down(f, owner):
            return send(block(f, owner), down_in.at[f, owner], down_send.at[f, owner],
                        down_recv.at[f, owner], here.along(line - 1), here.me)

        def add(f, owner, extra):
            rows = rows_of(owner, row_block)
            part_sum[f, rows] = part_sum[f, rows] + extra

        def up_add(f, owner):
            arrived(up_in.at[f, owner - 1], up_recv.at[f, owner - 1])
            add(f, owner, up_in[f, owner - 1])

        def down_add(f, owner):
            arrived(down_in.at[f, owner], down_recv.at[f, owner])
            add(f, owner, down_in[f, owner])

        def compute(f):
            for turn in range(8):
                arrived(got.at[f, turn], in_recv.at[f, turn])
            spectrum = split(got[f].reshape(16 * freq_block, freq_width))
            half = product((high[...], low[...]), spectrum)
            for part in range(2):
                lanes = slice(part * freq_width, (part + 1) * freq_width)
                half_high[:, lanes], half_low[:, lanes] = split(half[part * rows_all : (part + 1) * rows_all])
            part_sum[f] = product_across((half_high[...], half_low[...]), (to_cols[0], to_cols[1]))

        def relay(f, hop):
            high_end, low_end = line - hop, hop - 1

            @pl.when((at > 0) & (at < high_end))
            def _():
                up_add(f, high_end)

            @pl.when(at < high_end)
            def _():
                up(f, high_end).start()

            @pl.when((at < line - 1) & (at > low_end))
            def _():
                down_add(f, low_end)

            @pl.when(at > low_end)
            def _():
                down(f, low_end).start()

        def leave(f, turn):
            k, j = f // pair, f % pair
            src = turned.at[f, rows_of(here.peers[turn], col_block)]
            dst = image.at[k, here.me * pair + j]
            if turn == 0:
                return pltpu.make_async_copy(src, dst, out_send.at[f, 0])
            return send(src, dst, out_send.at[f, turn], out_recv.at[f, turn], at, here.peers[turn])

        def final(f):
            @pl.when(at > 0)
            def _():
                up_add(f, at)

            @pl.when(at < line - 1)
            def _():
                down_add(f, at)

            turned[f] = part_sum[f, rows_of(at, row_block)].T
            for turn in TURNS:
                leave(f, turn).start()

        for turn in range(1, 8):
            in_plane(turn).start()

        def step(f, carry):
            @pl.when(f < fields)
            def _():
                compute(f)
                relay(f, 1)

            @pl.when(f > 0)
            def _():
                final(f - 1)

            @pl.when(f < fields)
            def _():
                for hop in range(2, line):
                    relay(f, hop)

            return carry

        lax.fori_loop(0, fields + 1, step, 0)
        total = line_total[...]
        for turn in range(1, 8):
            in_plane(turn).wait()
            total = total + plane_sums[turn]
        totals[...] = total

        def finish(f, carry):
            leave(f, 0).wait()
            for turn in range(1, 8):
                leave(f, turn).wait()
            for owner in range(line):
                if owner > 0:
                    @pl.when(at < owner)
                    def _():
                        up(f, owner).wait_send()

                if owner < line - 1:
                    @pl.when(at > owner)
                    def _():
                        down(f, owner).wait_send()
            return carry

        lax.fori_loop(0, fields, finish, 0)
        for last in range(2):
            for j in range(pair):
                for turn in range(1, 8):
                    enter(last, j, turn).wait_send()

    dma = pltpu.SemaphoreType.DMA
    vmem = pl.BlockSpec(memory_space=pltpu.VMEM)
    hbm = pl.BlockSpec(memory_space=pl.ANY)
    hops = dma((fields, line - 1))
    stream = pltpu.VMEM((fields, line - 1, row_block, cols_all), jnp.float32)
    return pl.pallas_call(
        body,
        in_specs=[hbm, hbm, hbm, vmem, vmem, vmem, vmem, vmem],
        out_specs=[hbm, vmem, hbm],
        out_shape=[
            jax.ShapeDtypeStruct((rhs_count, seg_count, col_block, row_block), jnp.float32),
            jax.ShapeDtypeStruct(sums_shape, jnp.float32),
            jax.ShapeDtypeStruct(mixed.shape, jnp.float32),
        ],
        scratch_shapes=[
            pltpu.VMEM((fields, 8, 2, freq_block, freq_width), jnp.float32),
            pltpu.VMEM((fields, rows_all, cols_all), jnp.float32),
            pltpu.VMEM((2 * rows_all, 16 * freq_block), jnp.bfloat16),
            pltpu.VMEM((2 * rows_all, 16 * freq_block), jnp.bfloat16),
            pltpu.VMEM((rows_all, 2 * freq_width), jnp.bfloat16),
            pltpu.VMEM((rows_all, 2 * freq_width), jnp.bfloat16),
            stream, stream,
            pltpu.VMEM((fields, cols_all, row_block), jnp.float32),
            pltpu.VMEM(sums_shape, jnp.float32),
            pltpu.VMEM((line,) + sums_shape, jnp.float32),
            pltpu.VMEM(sums_shape, jnp.float32),
            pltpu.VMEM((8,) + sums_shape, jnp.float32),
            pltpu.VMEM(curve.shape, jnp.float32),
            dma((fields, 8)), dma((fields, 8)), hops, hops, hops, hops, dma((fields, 8)), dma((fields, 8)),
            dma((line,)), dma((line,)), dma((8,)), dma((8,)),
        ] + mix_scratch(symbol, seg_count, mix_step),
        compiler_params=pltpu.CompilerParams(
            collective_id=1, has_side_effects=True, vmem_limit_bytes=VMEM_LIMIT
        ),
        name="backward",
    )(symbol, spectra, mixed, norms, curve, fine, coarse, to_cols)


def halves(table):
    high = lax.reduce_precision(table, 8, 7)
    return jnp.stack([high, table - high]).astype(jnp.bfloat16)


def routed(right_side, symbol):
    line = lax.axis_size("row")
    rhs_count, seg_count, row_block, col_block = right_side.shape
    freq_block, freq_width = symbol.shape[:2]
    rows_all, cols_all = row_block * line, col_block * 8
    freq_rows, freq_cols = freq_block * 8, freq_width * line
    norm_factor = 1.0 / (freq_rows * freq_cols)
    owners = jnp.stack(Place(line).peers)
    fine = jnp.stack(tables(steps(freq_block)[:, None] * steps(rows_all)[None, :], freq_rows))
    coarse = jnp.stack(tables(owners[:, None] * steps(rows_all, freq_block)[None, :], freq_rows))
    to_cols = col_transform(freq_cols, cols_all, freq_width, lax.axis_index("row") * freq_width)
    norm_now = jnp.sum(right_side * right_side, axis=(1, 2, 3))
    norms = jnp.broadcast_to(norm_now[:, None], (rhs_count, 128))
    to_cols = halves(to_cols.transpose(1, 0, 2).reshape(cols_all, 2 * freq_width))
    spectra, mixed, curve = forward_call(right_side.transpose(0, 1, 3, 2), symbol, fine, coarse, to_cols, line)
    image, totals, _ = backward_call(
        symbol, spectra, mixed, norms, curve, fine, coarse, to_cols, line, row_block, col_block
    )
    applied = image.transpose(0, 1, 3, 2) * norm_factor
    step_size = (totals[0, :, 0] / (totals[1, :, 0] * norm_factor))[:, None, None, None]
    return (step_size * right_side, right_side - step_size * applied)


def fits(mesh, right_side, symbol):
    ring, wide = mesh.shape["row"], mesh.shape["col"]
    rhs_count, seg_count, rows, cols = right_side.shape
    freq_rows, freq_cols = symbol.shape[:2]
    aligned = all(n % 128 == 0 for n in (rows // ring, freq_rows // wide, freq_cols // ring))
    return ring > 1 and wide == 8 and rhs_count == 2 and seg_count % 8 == 0 and cols // wide % 8 == 0 and aligned


def solution(mesh):
    placed = P(None, None, "row", "col")

    def whole(right_side, symbol):
        return jax.shard_map(
            routed if fits(mesh, right_side, symbol) else local,
            mesh=mesh,
            in_specs=(placed, P("col", "row", None)),
            out_specs=(placed, placed),
            check_vma=False,
        )(right_side, symbol)

    return whole
```

```python
import math

import jax
import jax.numpy as jnp
from jax import lax
from jax.experimental import pallas as pl
from jax.experimental.pallas import tpu as pltpu
from jax.sharding import PartitionSpec as P

PRECISION = lax.Precision.HIGH
ROW_STEP = 8


def tables(phase, length):
    angle = (phase % length).astype(jnp.float32) * (2.0 * math.pi / length)
    return lax.optimization_barrier((jnp.cos(angle), jnp.sin(angle)))


def steps(count, stride=1):
    return jnp.arange(count, dtype=jnp.int32) * stride


def row_transform(freq_rows, rows_all, freq_block):
    fine = math.gcd(32, freq_block)
    place = jnp.tile(steps(rows_all), 2)
    part_in = jnp.repeat(steps(2), rows_all)
    coarse_cos, coarse_sin = tables(steps(freq_rows // fine, fine)[:, None] * place[None, :], freq_rows)
    quarter = (steps(2)[:, None] - part_in[None, :]) * (freq_rows // 4) + freq_rows
    fine_cos, fine_sin = tables(
        steps(fine)[None, :, None] * place[None, None, :] + quarter[:, None, :], freq_rows
    )
    shape = (freq_rows // freq_block, 1, freq_block // fine, 1, 2 * rows_all)
    coarse_cos, coarse_sin = coarse_cos.reshape(shape), coarse_sin.reshape(shape)
    fine_cos, fine_sin = fine_cos[None, :, None], fine_sin[None, :, None]
    return (coarse_cos * fine_cos - coarse_sin * fine_sin).reshape(2 * freq_rows, 2 * rows_all)


def col_transform(freq_cols, cols_all, freq_block, first):
    fine = math.gcd(16, cols_all)
    freq = first + steps(freq_block)
    coarse_cos, coarse_sin = tables(steps(cols_all // fine, fine)[:, None] * freq[None, :], freq_cols)
    quarter = steps(2, freq_cols // 4)[:, None, None]
    fine_cos, fine_sin = tables(steps(fine)[None, :, None] * freq[None, None, :] + quarter, freq_cols)
    coarse_cos, coarse_sin = coarse_cos[None, :, None], coarse_sin[None, :, None]
    fine_cos, fine_sin = fine_cos[:, None], fine_sin[:, None]
    return (coarse_cos * fine_cos - coarse_sin * fine_sin).reshape(2, cols_all, freq_block)


def mix(symbol, spectra, rhs_count, seg_count):
    freq_rows, freq_cols, pair_count = symbol.shape
    devices, parts, _, width = spectra[0].shape
    count = len(spectra)
    share = width // freq_cols
    step = math.gcd(ROW_STEP, freq_rows)

    def place(field):
        owner, at = divmod(field, share * count)
        group, at = divmod(at, share)
        return group, owner, slice(at * freq_cols, (at + 1) * freq_cols)

    def body(symbol_ref, *refs):
        in_refs, out_refs, turned = refs[:count], refs[count : 2 * count], refs[2 * count]

        def one(u, carry):
            turned[...] = symbol_ref[u].T
            sums = {}
            for t in range(seg_count):
                column = turned[t * seg_count : (t + 1) * seg_count, :]
                for part in range(parts):
                    for k in range(rhs_count):
                        group, owner, lanes = place(k * seg_count + t)
                        term = column * in_refs[group][owner, part, pl.ds(u, 1), lanes]
                        sums[part, k] = sums[part, k] + term if t else term
            for part in range(parts):
                for k in range(rhs_count):
                    for s in range(seg_count):
                        group, owner, lanes = place(k * seg_count + s)
                        out_refs[group][owner, part, pl.ds(u, 1), lanes] = sums[part, k][s : s + 1, :]
            return carry

        lax.fori_loop(0, step, one, 0)

    block = pl.BlockSpec((devices, parts, step, width), lambda i: (0, 0, i, 0))
    return pl.pallas_call(
        body,
        grid=(freq_rows // step,),
        in_specs=[pl.BlockSpec((step, freq_cols, pair_count), lambda i: (i, 0, 0))] + [block] * count,
        out_specs=[block] * count,
        out_shape=[jax.ShapeDtypeStruct(spectra[0].shape, jnp.float32)] * count,
        scratch_shapes=[pltpu.VMEM((pair_count, freq_cols), jnp.float32)],
        name="mix",
    )(symbol, *spectra)


def local(right_side, symbol):
    row_count = lax.axis_size("row")
    col_count = lax.axis_size("col")
    rhs_count, seg_count, row_block, col_block = right_side.shape
    freq_block, freq_width = symbol.shape[:2]
    rows_all = row_block * row_count
    cols_all = col_block * col_count
    freq_rows = freq_block * col_count
    freq_cols = freq_width * row_count
    fields = rhs_count * seg_count
    held = fields // col_count
    to_rows = row_transform(freq_rows, rows_all, freq_block)
    to_cols = col_transform(freq_cols, cols_all, freq_width, lax.axis_index("row") * freq_width)
    count = math.gcd(2, held)
    share = held // count
    norm_factor = 1.0 / (freq_rows * freq_cols)
    flat = right_side.reshape(fields, row_block, col_block)
    whole_cols = lax.all_to_all(flat, "col", split_axis=0, concat_axis=2, tiled=True)
    spectra = []
    for group in range(count):
        own = whole_cols[group * share : (group + 1) * share]
        whole = lax.all_gather(own, "row", axis=1, tiled=True)
        half = jnp.einsum("prc,zcv->zrpv", whole, to_cols, precision=PRECISION)
        half = half.reshape(2 * rows_all, share * freq_width)
        spectrum = jnp.dot(to_rows, half, precision=PRECISION)
        spectrum = spectrum.reshape(col_count, 2, freq_block, share * freq_width)
        spectra.append(lax.all_to_all(spectrum, "col", split_axis=0, concat_axis=0, tiled=True))
    mixtures = mix(symbol, spectra, rhs_count, seg_count)
    sums = []
    for spectrum, mixed in zip(spectra, mixtures):
        for at in range(share):
            lanes = slice(at * freq_width, (at + 1) * freq_width)
            sums.append(jnp.sum(spectrum[..., lanes] * mixed[..., lanes], axis=(1, 2, 3)))
    curve = jnp.stack(sums, axis=1).reshape(rhs_count, seg_count).sum(axis=1) * norm_factor
    norm_now = jnp.sum(right_side * right_side, axis=(1, 2, 3))
    norm_now, curve = lax.psum((norm_now, curve), ("row", "col"))
    images = []
    for mixed in mixtures:
        mixed = lax.all_to_all(mixed, "col", split_axis=0, concat_axis=0, tiled=True)
        mixed, norm_now, curve = lax.optimization_barrier((mixed, norm_now, curve))
        mixed = mixed.reshape(2 * freq_rows, share * freq_width)
        back = lax.dot_general(to_rows, mixed, (((0,), (0,)), ((), ())), precision=PRECISION)
        back = back.reshape(2, rows_all, share, freq_width)
        image = jnp.einsum("zrpv,zcv->prc", back, to_cols, precision=PRECISION)
        images.append(lax.psum_scatter(image, "row", scatter_dimension=1, tiled=True))
    image = jnp.concatenate(images, axis=0)
    applied = lax.all_to_all(image, "col", split_axis=2, concat_axis=0, tiled=True)
    applied = applied.reshape(right_side.shape) * norm_factor
    step_size = (norm_now / curve)[:, None, None, None]
    return (step_size * right_side, right_side - step_size * applied)


MESH = pl.DeviceIdType.MESH
VMEM_LIMIT = 60 * 1024 * 1024


def split(value):
    high = value.astype(jnp.bfloat16)
    return high, (value - high.astype(jnp.float32)).astype(jnp.bfloat16)


def product(left, right):
    def one(a, b):
        return jnp.dot(a, b, preferred_element_type=jnp.float32)

    return one(left[0], right[0]) + (one(left[1], right[0]) + one(left[0], right[1]))


def product_across(left, right):
    def one(a, b):
        return lax.dot_general(a, b, (((1,), (1,)), ((), ())), preferred_element_type=jnp.float32)

    return one(left[0], right[0]) + (one(left[1], right[0]) + one(left[0], right[1]))


def mix_scratch(symbol, seg_count, step):
    freq_rows, freq_cols, pair_count = symbol.shape
    block = pltpu.VMEM((2, seg_count, 2, step, freq_cols), jnp.float32)
    dma = pltpu.SemaphoreType.DMA
    return [
        pltpu.VMEM((2, step, freq_cols, pair_count), jnp.float32), block, block,
        pltpu.VMEM((pair_count, freq_cols), jnp.float32),
        dma((2,)), dma((2,)), dma((2,)),
    ]


def mix_one(symbol, spectra, mixed, curve, scratch):
    symbols, ins, outs, turned, symbol_sem, in_sem, out_sem = scratch
    seg_count, parts, freq_rows, _ = spectra.shape
    step = symbols.shape[1]
    count = freq_rows // step

    def load(c):
        rows, slot = rows_of(c, step), c % 2
        pltpu.make_async_copy(symbol.at[rows], symbols.at[slot], symbol_sem.at[slot]).start()
        pltpu.make_async_copy(spectra.at[:, :, rows], ins.at[slot], in_sem.at[slot]).start()

    def store(c):
        slot = c % 2
        return pltpu.make_async_copy(outs.at[slot], mixed.at[:, :, rows_of(c, step)], out_sem.at[slot])

    load(0)
    curve[...] = jnp.zeros_like(curve)

    def chunk(c, carry):
        slot = c % 2

        @pl.when(c + 1 < count)
        def _():
            load(c + 1)

        arrived(symbols.at[slot], symbol_sem.at[slot])
        arrived(ins.at[slot], in_sem.at[slot])

        @pl.when(c >= 2)
        def _():
            store(c - 2).wait()

        def one(u, inner):
            turned[...] = symbols[slot, u].T
            sums = [None] * parts
            for t in range(seg_count):
                column = turned[t * seg_count : (t + 1) * seg_count, :]
                for part in range(parts):
                    term = column * ins[slot, t, part, pl.ds(u, 1), :]
                    sums[part] = sums[part] + term if t else term
            for part in range(parts):
                for t in range(seg_count):
                    outs[slot, t, part, pl.ds(u, 1), :] = sums[part][t : t + 1, :]
            return inner

        lax.fori_loop(0, step, one, 0)
        total = curve[...]
        for t in range(seg_count):
            for part in range(parts):
                total = total + ins[slot, t, part] * outs[slot, t, part]
        curve[...] = total
        store(c).start()
        return carry

    lax.fori_loop(0, count, chunk, 0)
    store(count - 2).wait()
    store(count - 1).wait()


class Place:
    def __init__(self, line):
        self.line = line
        self.at, self.me = lax.axis_index("row"), lax.axis_index("col")
        bits = (self.me % 2, (self.me // 2) % 2, self.me // 4)
        self.peers = []
        for turn in range(8):
            flips = (turn % 2, (turn // 2) % 2, turn // 4)
            core, x, y = (bit + flip * (1 - 2 * bit) for bit, flip in zip(bits, flips))
            self.peers.append(y * 4 + x * 2 + core)

    def along(self, hops):
        return (self.at + hops) % self.line

    def greet(self):
        barrier = pltpu.get_barrier_semaphore()
        others = [(self.at, peer) for peer in self.peers[1:]]
        others += [(self.along(hops), self.me) for hops in range(1, self.line)]
        for other in others:
            pl.semaphore_signal(barrier, inc=1, device_id=other, device_id_type=MESH)
        pl.semaphore_wait(barrier, len(others))


def rows_of(at, size):
    return pl.ds(pl.multiple_of(at * size, size), size)


def arrived(ref, sem):
    pltpu.make_async_copy(ref, ref, sem).wait()


def send(src, dst, send_sem, recv_sem, row, col):
    return pltpu.make_async_remote_copy(
        src_ref=src, dst_ref=dst, send_sem=send_sem, recv_sem=recv_sem,
        device_id=(row, col), device_id_type=MESH,
    )


TURNS = (6, 2, 4, 7, 3, 5, 1, 0)


def backward_parts(here, sizes, operands, scratch):
    pair, fields, rows_all, row_block, col_block, freq_block, freq_width = sizes
    norms, fine, coarse, to_cols, mixed, mixed_last, curve, curve_last, image, totals = operands
    (got, part_sum, high, low, half_high, half_low, up_in, down_in, turned,
     scalars, line_sums, line_total, plane_sums,
     in_send, in_recv, up_send, up_recv, down_send, down_recv, out_send, out_recv,
     line_send, line_recv, plane_send, plane_recv) = scratch
    line, at = here.line, here.at

    def enter(last, j, turn):
        f = last * pair + j
        src = (mixed_last if last else mixed).at[here.peers[turn] * pair + j]
        dst = got.at[f, turn]
        if turn == 0:
            return pltpu.make_async_copy(src, dst, in_recv.at[f, 0])
        return send(src, dst, in_send.at[f, turn], in_recv.at[f, turn], at, here.peers[turn])

    def along_line(hops):
        return send(scalars, line_sums.at[hops], line_send.at[hops], line_recv.at[hops],
                    here.along(hops), here.me)

    def in_plane(turn):
        return send(line_total, plane_sums.at[turn], plane_send.at[turn], plane_recv.at[turn],
                    at, here.peers[turn])

    def begin(last):
        for j in range(pair):
            for turn in TURNS:
                enter(last, j, turn).start()

    def build(turn, carry):
        cos_c, sin_c = coarse[0, pl.ds(turn, 1), :], coarse[1, pl.ds(turn, 1), :]
        cos_f, sin_f = fine[0], fine[1]
        cos = split((cos_c * cos_f - sin_c * sin_f).T)
        sin = split((sin_c * cos_f + cos_c * sin_f).T)
        for part, table in ((0, high), (1, low)):
            for half in range(2):
                lanes = rows_of(turn * 2 + half, freq_block)
                table[:rows_all, lanes] = -sin[part] if half else cos[part]
                table[rows_all:, lanes] = cos[part] if half else sin[part]
        return carry

    def share():
        scalars[0] = norms[...]
        for k, part in ((0, curve), (1, curve_last)):
            whole = jnp.sum(jnp.sum(part[...], axis=0, keepdims=True), axis=1, keepdims=True)
            scalars[1, k : k + 1, :] = jnp.broadcast_to(whole, (1, norms.shape[1]))
        for hops in range(1, line):
            along_line(hops).start()

    def share_plane():
        total = scalars[...]
        for hops in range(1, line):
            along_line(hops).wait()
            total = total + line_sums[hops]
        line_total[...] = total
        for turn in range(1, 8):
            in_plane(turn).start()

    def block(f, owner):
        return part_sum.at[f, rows_of(owner, row_block)]

    def up(f, owner):
        return send(block(f, owner), up_in.at[f, owner - 1], up_send.at[f, owner - 1],
                    up_recv.at[f, owner - 1], here.along(1), here.me)

    def down(f, owner):
        return send(block(f, owner), down_in.at[f, owner], down_send.at[f, owner],
                    down_recv.at[f, owner], here.along(line - 1), here.me)

    def add(f, owner, extra):
        rows = rows_of(owner, row_block)
        part_sum[f, rows] = part_sum[f, rows] + extra

    def up_add(f, owner):
        arrived(up_in.at[f, owner - 1], up_recv.at[f, owner - 1])
        add(f, owner, up_in[f, owner - 1])

    def down_add(f, owner):
        arrived(down_in.at[f, owner], down_recv.at[f, owner])
        add(f, owner, down_in[f, owner])

    def compute(f):
        for turn in range(8):
            arrived(got.at[f, turn], in_recv.at[f, turn])
        spectrum = split(got[f].reshape(16 * freq_block, freq_width))
        half = product((high[...], low[...]), spectrum)
        for part in range(2):
            lanes = slice(part * freq_width, (part + 1) * freq_width)
            half_high[:, lanes], half_low[:, lanes] = split(half[part * rows_all : (part + 1) * rows_all])
        part_sum[f] = product_across((half_high[...], half_low[...]), (to_cols[0], to_cols[1]))

    def relay(f, hop):
        high_end, low_end = line - hop, hop - 1

        @pl.when((at > 0) & (at < high_end))
        def _():
            up_add(f, high_end)

        @pl.when(at < high_end)
        def _():
            up(f, high_end).start()

        @pl.when((at < line - 1) & (at > low_end))
        def _():
            down_add(f, low_end)

        @pl.when(at > low_end)
        def _():
            down(f, low_end).start()

    def leave(f, turn):
        k, j = f // pair, f % pair
        src = turned.at[f, rows_of(here.peers[turn], col_block)]
        dst = image.at[k, here.me * pair + j]
        if turn == 0:
            return pltpu.make_async_copy(src, dst, out_send.at[f, 0])
        return send(src, dst, out_send.at[f, turn], out_recv.at[f, turn], at, here.peers[turn])

    def final(f):
        @pl.when(at > 0)
        def _():
            up_add(f, at)

        @pl.when(at < line - 1)
        def _():
            down_add(f, at)

        turned[f] = part_sum[f, rows_of(at, row_block)].T
        for turn in TURNS:
            leave(f, turn).start()

    def step(f, carry):
        @pl.when(f < fields)
        def _():
            compute(f)
            relay(f, 1)

        @pl.when(f > 0)
        def _():
            final(f - 1)

        @pl.when(f < fields)
        def _():
            for hop in range(2, line):
                relay(f, hop)

        return carry

    def run():
        lax.fori_loop(0, fields + 1, step, 0)
        total = line_total[...]
        for turn in range(1, 8):
            in_plane(turn).wait()
            total = total + plane_sums[turn]
        totals[...] = total

    def finish(f, carry):
        leave(f, 0).wait()
        for turn in range(1, 8):
            leave(f, turn).wait()
        for owner in range(line):
            if owner > 0:
                @pl.when(at < owner)
                def _():
                    up(f, owner).wait_send()

            if owner < line - 1:
                @pl.when(at > owner)
                def _():
                    down(f, owner).wait_send()
        return carry

    def done():
        lax.fori_loop(0, fields, finish, 0)
        for last in range(2):
            for j in range(pair):
                for turn in range(1, 8):
                    enter(last, j, turn).wait_send()

    return begin, lambda: lax.fori_loop(0, 8, build, 0), share, share_plane, run, done


def operate_call(packed, symbol, norms, fine, coarse, to_cols, line):
    freq_block, freq_width = symbol.shape[:2]
    mix_step = math.gcd(ROW_STEP, freq_block)
    rhs_count, seg_count, col_block, row_block = packed.shape
    pair = seg_count // 8
    fields = rhs_count * pair
    rows_all, cols_all = row_block * line, col_block * 8

    def body(packed, symbol, norms, fine, coarse, to_cols, image, totals, spec, mixed, mixed_last, *scratch):
        (stage, pix, high, low, half_high, half_low, out, curve, curve_last,
         in_send, in_recv, up_send, up_recv, down_send, down_recv, out_send, out_recv) = scratch[:17]
        mix_refs, back_refs = scratch[17:24], scratch[24:]
        here = Place(line)
        at = here.at
        here.greet()
        begin, build_back, share, share_plane, run, done = backward_parts(
            here, (pair, fields, rows_all, row_block, col_block, freq_block, freq_width),
            (norms, fine, coarse, to_cols, mixed, mixed_last, curve, curve_last, image, totals), back_refs,
        )

        def first(f, turn):
            k, j = f // pair, f % pair
            src = packed.at[k, here.peers[turn] * pair + j]
            dst = stage.at[f, rows_of(here.me, col_block)]
            if turn == 0:
                return pltpu.make_async_copy(src, dst, in_recv.at[f])
            return send(src, dst, in_send.at[f, turn], in_recv.at[f], at, here.peers[turn])

        for f in range(fields):
            for turn in TURNS:
                first(f, turn).start()

        def build(turn, carry):
            cos_c, sin_c = coarse[0, pl.ds(turn, 1), :], coarse[1, pl.ds(turn, 1), :]
            cos_f, sin_f = fine[0], fine[1]
            cos = split(cos_c * cos_f - sin_c * sin_f)
            sin = split(sin_c * cos_f + cos_c * sin_f)
            for part, table in ((0, high), (1, low)):
                table[turn, :freq_block, :rows_all] = cos[part]
                table[turn, :freq_block, rows_all:] = sin[part]
                table[turn, freq_block:, :rows_all] = -sin[part]
                table[turn, freq_block:, rows_all:] = cos[part]
            return carry

        def block(f, owner):
            return pix.at[f, rows_of(owner, row_block)]

        def up(f, hop):
            own = block(f, here.along(line - hop))
            return send(own, own, up_send.at[f, hop], up_recv.at[f, hop], here.along(1), here.me)

        def down(f, hop):
            own = block(f, here.along(hop))
            return send(own, own, down_send.at[f, hop], down_recv.at[f, hop], here.along(line - 1), here.me)

        def up_goes(hop):
            return (at >= hop) & (at < line - 1)

        def down_goes(hop):
            return (at < line - hop) & (at > 0)

        def enter(f):
            arrived(stage.at[f], in_recv.at[f])
            pix[f, rows_of(at, row_block)] = stage[f].T

            @pl.when(up_goes(0))
            def _():
                up(f, 0).start()

            @pl.when(down_goes(0))
            def _():
                down(f, 0).start()

        def relay(f, hop):
            @pl.when(at >= hop)
            def _():
                arrived(block(f, here.along(line - hop)), up_recv.at[f, hop - 1])

            if hop < line - 1:
                @pl.when(up_goes(hop))
                def _():
                    up(f, hop).start()

            @pl.when(at < line - hop)
            def _():
                arrived(block(f, here.along(hop)), down_recv.at[f, hop - 1])

            if hop < line - 1:
                @pl.when(down_goes(hop))
                def _():
                    down(f, hop).start()

        def leave(f, turn):
            k, j = f // pair, f % pair
            src = out.at[f % 2, turn]
            dst = spec.at[k, here.me * pair + j]
            if turn == 0:
                return pltpu.make_async_copy(src, dst, out_send.at[f, 0])
            return send(src, dst, out_send.at[f, turn], out_recv.at[f, turn], at, here.peers[turn])

        def sent(f):
            leave(f, 0).wait()
            for turn in range(1, 8):
                leave(f, turn).wait_send()

        def compute(f):
            half = product(split(pix[f]), (to_cols[0], to_cols[1]))
            for part in range(2):
                rows = slice(part * rows_all, (part + 1) * rows_all)
                half_high[rows, :], half_low[rows, :] = split(half[:, part * freq_width : (part + 1) * freq_width])

            @pl.when(f >= 2)
            def _():
                sent(f - 2)

            right = (half_high[...], half_low[...])
            for turn in TURNS:
                value = product((high[turn], low[turn]), right)
                out[f % 2, turn] = value.reshape(2, freq_block, freq_width)
                leave(f, turn).start()

        enter(0)
        lax.fori_loop(0, 8, build, 0)

        def step(f, carry):
            for hop in range(1, line - 1):
                relay(f, hop)

            @pl.when(f + 1 < fields)
            def _():
                enter(f + 1)

            relay(f, line - 1)
            compute(f)
            return carry

        lax.fori_loop(0, fields, step, 0)

        def landed(f, carry):
            for turn in range(1, 8):
                leave(f, turn).wait_recv()
            return carry

        lax.fori_loop(0, pair, landed, 0)
        mix_one(symbol, spec.at[0], mixed, curve, mix_refs)
        begin(0)
        build_back()
        lax.fori_loop(pair, fields, landed, 0)
        sent(fields - 2)
        sent(fields - 1)
        mix_one(symbol, spec.at[1], mixed_last, curve_last, mix_refs)
        begin(1)
        share()
        share_plane()
        run()

        def finish(f, carry):
            for turn in range(1, 8):
                first(f, turn).wait_send()
            for hop in range(line - 1):
                @pl.when(up_goes(hop))
                def _():
                    up(f, hop).wait_send()

                @pl.when(down_goes(hop))
                def _():
                    down(f, hop).wait_send()
            return carry

        lax.fori_loop(0, fields, finish, 0)
        done()

    dma = pltpu.SemaphoreType.DMA
    vmem = pl.BlockSpec(memory_space=pltpu.VMEM)
    hbm = pl.BlockSpec(memory_space=pl.ANY)
    hops = dma((fields, line - 1))
    stream = pltpu.VMEM((fields, line - 1, row_block, cols_all), jnp.float32)
    sums_shape = (2,) + norms.shape
    mixture = jax.ShapeDtypeStruct((seg_count, 2, freq_block, freq_width), jnp.float32)
    table = pltpu.VMEM((8, 2 * freq_block, 2 * rows_all), jnp.bfloat16)
    back_table = pltpu.VMEM((2 * rows_all, 16 * freq_block), jnp.bfloat16)
    half = pltpu.VMEM((2 * rows_all, freq_width), jnp.bfloat16)
    back_half = pltpu.VMEM((rows_all, 2 * freq_width), jnp.bfloat16)
    plane = pltpu.VMEM((fields, cols_all, row_block), jnp.float32)
    pixels = pltpu.VMEM((fields, rows_all, cols_all), jnp.float32)
    curves = pltpu.VMEM((mix_step, freq_width), jnp.float32)
    peers = dma((fields, 8))
    forward_scratch = [
        plane, pixels, table, table, half, half,
        pltpu.VMEM((2, 8, 2, freq_block, freq_width), jnp.float32), curves, curves,
        peers, dma((fields,)), hops, hops, hops, hops, peers, peers,
    ]
    backward_scratch = [
        pltpu.VMEM((fields, 8, 2, freq_block, freq_width), jnp.float32),
        pixels, back_table, back_table, back_half, back_half, stream, stream, plane,
        pltpu.VMEM(sums_shape, jnp.float32),
        pltpu.VMEM((line,) + sums_shape, jnp.float32),
        pltpu.VMEM(sums_shape, jnp.float32),
        pltpu.VMEM((8,) + sums_shape, jnp.float32),
        peers, peers, hops, hops, hops, hops, peers, peers,
        dma((line,)), dma((line,)), dma((8,)), dma((8,)),
    ]
    return pl.pallas_call(
        body,
        in_specs=[hbm, hbm, vmem, vmem, vmem, vmem],
        out_specs=[hbm, vmem, hbm, hbm, hbm],
        out_shape=[
            jax.ShapeDtypeStruct(packed.shape, jnp.float32),
            jax.ShapeDtypeStruct(sums_shape, jnp.float32),
            jax.ShapeDtypeStruct((rhs_count,) + mixture.shape, jnp.float32),
            mixture, mixture,
        ],
        scratch_shapes=forward_scratch + mix_scratch(symbol, seg_count, mix_step) + backward_scratch,
        compiler_params=pltpu.CompilerParams(
            collective_id=0, has_side_effects=True, vmem_limit_bytes=VMEM_LIMIT
        ),
        name="operate",
    )(packed, symbol, norms, fine, coarse, to_cols)


def halves(table):
    high = lax.reduce_precision(table, 8, 7)
    return jnp.stack([high, table - high]).astype(jnp.bfloat16)


def routed(right_side, symbol):
    line = lax.axis_size("row")
    rhs_count, seg_count, row_block, col_block = right_side.shape
    freq_block, freq_width = symbol.shape[:2]
    rows_all, cols_all = row_block * line, col_block * 8
    freq_rows, freq_cols = freq_block * 8, freq_width * line
    norm_factor = 1.0 / (freq_rows * freq_cols)
    owners = jnp.stack(Place(line).peers)
    fine = jnp.stack(tables(steps(freq_block)[:, None] * steps(rows_all)[None, :], freq_rows))
    coarse = jnp.stack(tables(owners[:, None] * steps(rows_all, freq_block)[None, :], freq_rows))
    to_cols = col_transform(freq_cols, cols_all, freq_width, lax.axis_index("row") * freq_width)
    norm_now = jnp.sum(right_side * right_side, axis=(1, 2, 3))
    norms = jnp.broadcast_to(norm_now[:, None], (rhs_count, 128))
    to_cols = halves(to_cols.transpose(1, 0, 2).reshape(cols_all, 2 * freq_width))
    packed = right_side.transpose(0, 1, 3, 2)
    image, totals, _, _, _ = operate_call(packed, symbol, norms, fine, coarse, to_cols, line)
    applied = image.transpose(0, 1, 3, 2) * norm_factor
    step_size = (totals[0, :, 0] / (totals[1, :, 0] * norm_factor))[:, None, None, None]
    return (step_size * right_side, right_side - step_size * applied)


def fits(mesh, right_side, symbol):
    ring, wide = mesh.shape["row"], mesh.shape["col"]
    rhs_count, seg_count, rows, cols = right_side.shape
    freq_rows, freq_cols = symbol.shape[:2]
    aligned = all(n % 128 == 0 for n in (rows // ring, freq_rows // wide, freq_cols // ring))
    return ring > 1 and wide == 8 and rhs_count == 2 and seg_count % 16 == 0 and cols // wide % 8 == 0 and aligned


def solution(mesh):
    placed = P(None, None, "row", "col")

    def whole(right_side, symbol):
        return jax.shard_map(
            routed if fits(mesh, right_side, symbol) else local,
            mesh=mesh,
            in_specs=(placed, P("col", "row", None)),
            out_specs=(placed, placed),
            check_vma=False,
        )(right_side, symbol)

    return whole
```
